32 devices in a mesh: dp: 16 (over z, y, x), seq: 2 (over core).
Axes of the slice: x: 2, y: 2, z: 4, core: 2. Of those that a mesh axis runs over, the one named last changes fastest.
Arguments:
- tokens: bfloat16 [32, 1024, 768], P('dp', 'seq'), may hold values from -6 to 6
- segments: int32 [32, 1024], P('dp'), may hold values from 0 to 7, never falling along the last dimension, each value on 1 to 256 neighbouring positions
- query_weight: bfloat16 [768, 768], replicated, may hold values from -0.21875 to 0.21875
- query_bias: bfloat16 [768], replicated, may hold values from -1.75 to 1.75
- key_weight: bfloat16 [768, 768], replicated, may hold values from -0.21875 to 0.21875
- value_weight: bfloat16 [768, 768], replicated, may hold values from -0.21875 to 0.21875
- value_bias: bfloat16 [768], replicated, may hold values from -1.75 to 1.75
- output_weight: bfloat16 [768, 768], replicated, may hold values from -0.875 to 0.875
- output_bias: bfloat16 [768], replicated, may hold values from -1.75 to 1.75
- first_gain: bfloat16 [768], replicated, may hold values from 0.099609375 to 1.8984375
- first_shift: bfloat16 [768], replicated, may hold values from -1.75 to 1.75
- inner_weight: bfloat16 [768, 3072], replicated, may hold values from -0.21875 to 0.21875
- inner_bias: bfloat16 [3072], replicated, may hold values from -1.75 to 1.75
- outer_weight: bfloat16 [3072, 768], replicated, may hold values from -0.109375 to 0.109375
- outer_bias: bfloat16 [768], replicated, may hold values from -1.75 to 1.75
- second_gain: bfloat16 [768], replicated, may hold values from 0.099609375 to 1.8984375
- second_shift: bfloat16 [768], replicated, may hold values from -1.75 to 1.75
- cotangent: bfloat16 [32, 1024, 768], P('dp', 'seq'), may hold values from -6 to 6
Outputs:
- layer_out: bfloat16 [32, 1024, 768], P('dp', 'seq')
- tokens_grad: bfloat16 [32, 1024, 768], P('dp', 'seq')
- query_weight_grad: float32 [768, 768], P('dp')
- query_bias_grad: float32 [768], P('dp')
- key_weight_grad: float32 [768, 768], P('dp')
- value_weight_grad: float32 [768, 768], P('dp')
- value_bias_grad: float32 [768], P('dp')
- output_weight_grad: float32 [768, 768], P('dp')
- output_bias_grad: float32 [768], P('dp')
- first_gain_grad: float32 [768], P('dp')
- first_shift_grad: float32 [768], P('dp')
- inner_weight_grad: float32 [768, 3072], P('dp')
- inner_bias_grad: float32 [3072], P('dp')
- outer_weight_grad: float32 [3072, 768], P('dp')
- outer_bias_grad: float32 [768], P('dp')
- second_gain_grad: float32 [768], P('dp')
- second_shift_grad: float32 [768], P('dp')
The draws below stay inside these ranges and needn't reach their ends.
Inputs may be any that keep to these rules, and one draw needn't show every extreme that they name: `segments`: along each row the ids never fall and every id appears; each id covers at most 256 positions; the positions with id 8 - 1 are padding.
All inputs are finite; a program needn't handle non-finite values.
Results may differ from the reference program's by a relative error of at most 0.015.
Values may be sent and summed in bfloat16 or wider, within the bound.
No kernel may reach another device: no remote copies, remote signals or barrier semaphores. Data moves between devices by JAX's collectives and lax.ppermute only.
A program may use at most 192 MiB of HBM per device.

```python
import math
import jax
import jax.numpy as jnp
import numpy as np
from jax import lax

D = 768
HEADS = 12
HEAD_DIM = 64
FF = 3072
LEN = 1024
DOCS = 8
MOST = 256
ROWS = 32


def levels(rng, dims, cuts, smallest, top_value):
    def one(position, blocks):
        heights = jax.random.uniform(jax.random.fold_in(jax.random.fold_in(rng, 6), position), (blocks,), jnp.float32, smallest / len(cuts), top_value / len(cuts))
        return jnp.repeat(jnp.exp(heights), dims[position] // blocks).reshape((-1,) + (1,) * (len(dims) - position - 1))

    level = one(*cuts[0])
    for cut in cuts[1:]:
        level = level * one(*cut)
    return level


def profile(amount, total, bound, slope):
    loads = [(1 << 20) // math.isqrt(standing ** slope) + 1 for standing in range(2, amount + 1)]
    spare, holding = total - bound - (amount - 1), [1] * (amount - 1)
    while spare > 0:
        candidates = [i for i in range(amount - 1) if holding[i] < bound]
        whole, budget = sum([loads[i] for i in candidates]), spare
        for i in candidates:
            extra = min(bound - holding[i], max(1, budget * loads[i] // whole), spare)
            holding[i] = holding[i] + extra
            spare = spare - extra
    return np.array([bound] + holding)


def uneven_parts(rng, amount, total, bound, skew):
    if amount == 2:
        one = jax.random.randint(rng, (), max(1, total - bound), min(bound, total - 1) + 1)
        return jnp.stack([one, total - one])
    sizes = jnp.asarray(profile(amount, total, bound, skew), jnp.int32)
    twos = (amount - 1) // 2
    giver, sink = sizes[1:1 + 2 * twos:2], sizes[2:2 + 2 * twos:2]
    room = jnp.minimum(giver - 1, bound - sink)
    moved = jax.random.randint(jax.random.fold_in(rng, 1), (twos,), 0, 1 << 20) % (room + 1)
    sizes = sizes.at[1:1 + 2 * twos:2].set(giver - moved).at[2:2 + 2 * twos:2].set(sink + moved)
    return sizes[jax.random.permutation(jax.random.fold_in(rng, 2), amount)]


def normal_values(stream_key, shape, scale, bound, cuts=(), held_as=jnp.bfloat16):
    level = levels(stream_key, shape, cuts, -0.22, 0.18) if cuts else 1.0
    result = jax.random.normal(stream_key, shape, jnp.float32) * scale * level
    return jnp.minimum(jnp.maximum(result, -bound), bound).astype(held_as)


def setup_inputs(seed: int = 0) -> dict:
    seeds = jax.random.split(jax.random.key(seed), 19)
    return {
        "tokens": normal_values(seeds[0], (ROWS, LEN, D), 1.0, 6.0, ((0, 16), (1, 2))),
        "segments": jax.vmap(lambda own: jnp.searchsorted(jnp.cumsum(uneven_parts(own, DOCS, LEN, MOST, 2)), jnp.arange(LEN), side="right"))(jax.random.split(seeds[1], ROWS)).reshape((ROWS, LEN)).astype(jnp.int32),
        "query_weight": normal_values(seeds[2], (D, D), D ** -0.5, 0.21875),
        "query_bias": normal_values(seeds[3], (D,), 0.3, 1.75),
        "key_weight": normal_values(seeds[4], (D, D), D ** -0.5, 0.21875),
        "value_weight": normal_values(seeds[5], (D, D), D ** -0.5, 0.21875),
        "value_bias": normal_values(seeds[6], (D,), 0.3, 1.75),
        "output_weight": normal_values(seeds[7], (D, D), (D // 16) ** -0.5, 0.875),
        "output_bias": normal_values(seeds[8], (D,), 0.3, 1.75),
        "first_gain": jnp.clip(1.0 + 0.18 * jax.random.normal(seeds[9], (D,), jnp.float32), 0.099609375, 1.8984375).astype(jnp.bfloat16),
        "first_shift": normal_values(seeds[10], (D,), 0.3, 1.75),
        "inner_weight": normal_values(seeds[11], (D, FF), D ** -0.5, 0.21875),
        "inner_bias": normal_values(seeds[12], (FF,), 0.3, 1.75),
        "outer_weight": normal_values(seeds[13], (FF, D), FF ** -0.5, 0.109375),
        "outer_bias": normal_values(seeds[14], (D,), 0.3, 1.75),
        "second_gain": jnp.clip(1.0 + 0.18 * jax.random.normal(seeds[15], (D,), jnp.float32), 0.099609375, 1.8984375).astype(jnp.bfloat16),
        "second_shift": normal_values(seeds[16], (D,), 0.3, 1.75),
        "cotangent": normal_values(seeds[17], (ROWS, LEN, D), 1.0, 6.0, ((0, 16), (1, 2))),
    }


@jax.custom_vjp
def low(v):
    return lax.optimization_barrier(v.astype(jnp.bfloat16)).astype(jnp.float32)

@jax.custom_vjp
def low_back(v):
    return v

def low_keep(v):
    return (low(v), None)

def low_pass(kept, grad):
    return (grad,)

def back_keep(v):
    return (v, None)

def back_low(kept, grad):
    return (low(grad),)
low.defvjp(low_keep, low_pass)
low_back.defvjp(back_keep, back_low)

def matmul(left, right):
    return jnp.dot(left, right, precision=lax.Precision.HIGHEST)

def layer_norm(summed, gain, shift):
    centre = summed - lax.optimization_barrier(jnp.mean(summed, axis=-1, keepdims=True))
    spread = lax.optimization_barrier(jnp.mean(centre * centre, axis=-1, keepdims=True))
    return centre * lax.rsqrt(spread + 1e-12) * gain + shift

def forward_row(inputs, segment_row, params):
    query_weight, query_bias, key_weight, value_weight, value_bias, output_weight, output_bias, first_gain, first_shift, inner_weight, inner_bias, outer_weight, outer_bias, second_gain, second_shift = params
    length = inputs.shape[0]
    query = low(low_back(matmul(inputs, query_weight) + query_bias))
    key = low(low_back(matmul(inputs, key_weight)))
    value = low(low_back(matmul(inputs, value_weight) + value_bias))
    heads_query = query.reshape(length, HEADS, HEAD_DIM)
    heads_key = key.reshape(length, HEADS, HEAD_DIM)
    heads_value = value.reshape(length, HEADS, HEAD_DIM)
    scores = low_back(jnp.einsum('qhd,khd->hqk', heads_query, heads_key, precision=lax.Precision.HIGHEST) * 0.125)
    valid = segment_row != DOCS - 1
    allowed = (segment_row[:, None] == segment_row[None, :]) & valid[:, None] & valid[None, :]
    masked = jnp.where(allowed[None], scores, -jnp.inf)
    largest = lax.optimization_barrier(jnp.max(masked, axis=-1))
    safe_max = jnp.where(valid[None, :], largest, 0.0)
    weights = jnp.exp(jnp.where(allowed[None], scores - safe_max[..., None], -jnp.inf))
    total = lax.optimization_barrier(jnp.sum(weights, axis=-1))
    safe_total = jnp.where(valid[None, :], total, 1.0)
    probs = low(weights / safe_total[..., None])
    context = jnp.einsum('hqk,khd->qhd', probs, heads_value, precision=lax.Precision.HIGHEST)
    context = low(low_back(context.reshape(length, HEADS * HEAD_DIM)))
    attended = low_back(matmul(context, output_weight) + output_bias)
    first_norm = layer_norm(inputs + attended, first_gain, first_shift)
    norm_low = low(first_norm)
    inner = low_back(matmul(norm_low, inner_weight) + inner_bias)
    act = low(jax.nn.gelu(inner, approximate=False))
    outer = low_back(matmul(act, outer_weight) + outer_bias)
    return layer_norm(first_norm + outer, second_gain, second_shift)

def reference(tokens, segments, query_weight, query_bias, key_weight, value_weight, value_bias, output_weight, output_bias, first_gain, first_shift, inner_weight, inner_bias, outer_weight, outer_bias, second_gain, second_shift, cotangent):
    params = (query_weight.astype(jnp.float32), query_bias.astype(jnp.float32), key_weight.astype(jnp.float32), value_weight.astype(jnp.float32), value_bias.astype(jnp.float32), output_weight.astype(jnp.float32), output_bias.astype(jnp.float32), first_gain.astype(jnp.float32), first_shift.astype(jnp.float32), inner_weight.astype(jnp.float32), inner_bias.astype(jnp.float32), outer_weight.astype(jnp.float32), outer_bias.astype(jnp.float32), second_gain.astype(jnp.float32), second_shift.astype(jnp.float32))
    inputs = tokens.astype(jnp.float32)
    grad_in = cotangent.astype(jnp.float32)
    zeros = tuple((jnp.zeros(param.shape, jnp.float32) for param in params))

    def step(carry, item):
        input_row, segment_row, grad_row = item

        def apply(row_value, param_set):
            return forward_row(row_value, segment_row, param_set)
        out_row, backward = jax.vjp(apply, input_row, params)
        row_grad, param_grads = backward(grad_row)
        carry = tuple((total + term for total, term in zip(carry, param_grads)))
        return (carry, (out_row.astype(jnp.bfloat16), row_grad.astype(jnp.bfloat16)))
    totals, (outputs, input_grads) = lax.scan(step, zeros, (inputs, segments, grad_in))
    return (outputs, input_grads, totals[0], totals[1], totals[2], totals[3], totals[4], totals[5], totals[6], totals[7], totals[8], totals[9], totals[10], totals[11], totals[12], totals[13], totals[14])
```

```python
import jax
import jax.numpy as jnp
from jax import lax
from jax.sharding import PartitionSpec as P

HEAD_DIM = 64
DOCS = 8
SWAP = [(0, 1), (1, 0)]


def layer_norm(summed, gain, shift):
    centre = summed - jnp.mean(summed, axis=-1, keepdims=True)
    spread = jnp.mean(centre * centre, axis=-1, keepdims=True)
    return centre * lax.rsqrt(spread + 1e-12) * gain + shift


def gelu_exact(inner):
    return jax.nn.gelu(inner, approximate=False)


def dense(left, right):
    return jnp.dot(left, right, preferred_element_type=jnp.float32)


def block_scores(query_block, heads_key, segment_block, segment_row):
    valid_keys = segment_row != DOCS - 1
    valid_block = segment_block != DOCS - 1
    allowed = (
        (segment_block[:, None] == segment_row[None, :])
        & valid_block[:, None]
        & valid_keys[None, :]
    )
    scores = (
        jnp.einsum("qhd,khd->hqk", query_block, heads_key, preferred_element_type=jnp.float32)
        * 0.125
    )
    return (scores, allowed[None], valid_block)


def attend_forward(item):
    query, key, value, segment_row = item
    length, local = query.shape
    heads = local // HEAD_DIM
    block = min(512, length)
    heads_query = query.reshape(length, heads, HEAD_DIM)
    heads_key = key.reshape(length, heads, HEAD_DIM)
    heads_value = value.reshape(length, heads, HEAD_DIM)
    pieces = []
    sums = []
    for start in range(0, length, block):
        scores, allowed, valid_block = block_scores(
            heads_query[start : start + block],
            heads_key,
            segment_row[start : start + block],
            segment_row,
        )
        largest = jnp.max(jnp.where(allowed, scores, -jnp.inf), axis=-1)
        safe_max = jnp.where(valid_block[None, :], largest, 0.0)
        weights = jnp.exp(jnp.where(allowed, scores - safe_max[..., None], -jnp.inf))
        total = jnp.sum(weights, axis=-1)
        safe_total = jnp.where(valid_block[None, :], total, 1.0)
        probs = (weights / safe_total[..., None]).astype(jnp.bfloat16)
        context = jnp.einsum("hqk,khd->qhd", probs, heads_value, preferred_element_type=jnp.float32)
        pieces.append(context.reshape(block, local).astype(jnp.bfloat16))
        sums.append(safe_max + jnp.log(safe_total))
    return (jnp.concatenate(pieces, axis=0), jnp.concatenate(sums, axis=1))


def attend_backward(item):
    query, key, value, segment_row, grad_context, logsum = item
    length, local = query.shape
    heads = local // HEAD_DIM
    block = min(512, length)
    heads_query = query.reshape(length, heads, HEAD_DIM)
    heads_key = key.reshape(length, heads, HEAD_DIM)
    heads_value = value.reshape(length, heads, HEAD_DIM)
    grad_key = jnp.zeros((length, heads, HEAD_DIM), jnp.float32)
    grad_value = jnp.zeros((length, heads, HEAD_DIM), jnp.float32)
    query_pieces = []
    for start in range(0, length, block):
        query_block = heads_query[start : start + block]
        scores, allowed, valid_block = block_scores(
            query_block, heads_key, segment_row[start : start + block], segment_row
        )
        probs = jnp.exp(
            jnp.where(allowed, scores - logsum[:, start : start + block][..., None], -jnp.inf)
        )
        probs_low = probs.astype(jnp.bfloat16)
        grad_block = grad_context[start : start + block].reshape(block, heads, HEAD_DIM)
        grad_probs = jnp.einsum(
            "qhd,khd->hqk", grad_block, heads_value, preferred_element_type=jnp.float32
        )
        grad_value = grad_value + jnp.einsum(
            "hqk,qhd->khd", probs_low, grad_block, preferred_element_type=jnp.float32
        )
        inner = jnp.sum(grad_probs * probs, axis=-1, keepdims=True)
        grad_scores = (probs * (grad_probs - inner)).astype(jnp.bfloat16)
        query_grad = (
            jnp.einsum("hqk,khd->qhd", grad_scores, heads_key, preferred_element_type=jnp.float32)
            * 0.125
        )
        query_pieces.append(query_grad.reshape(block, local).astype(jnp.bfloat16))
        grad_key = (
            grad_key
            + jnp.einsum(
                "hqk,qhd->khd", grad_scores, query_block, preferred_element_type=jnp.float32
            )
            * 0.125
        )
    return (
        jnp.concatenate(query_pieces, axis=0),
        grad_key.reshape(length, local).astype(jnp.bfloat16),
        grad_value.reshape(length, local).astype(jnp.bfloat16),
    )


def pick(array, index, axis):
    return lax.dynamic_index_in_dim(array, index, axis, keepdims=False)


def total_of(parts):
    result = parts[0].astype(jnp.float32)
    for part in parts[1:]:
        result = result + part.astype(jnp.float32)
    return result


def scatter_sum(term, order):
    size = lax.axis_size("dp")
    me = lax.axis_index("dp")
    core = lax.axis_index("seq")
    bits = size.bit_length() - 1
    rows, columns = term.shape
    own = rows // size // 2
    term = term.reshape((2,) * bits + (2, own, columns))
    sent = pick(term, 1 - core, bits).astype(jnp.bfloat16)
    parts = [pick(term, core, bits), lax.ppermute(sent, "seq", SWAP)]
    left = list(range(bits - 1, -1, -1))
    for bit in [b for b in order if b < bits] + [b for b in range(bits) if b not in order]:
        axis = left.index(bit)
        mine = (me >> bit) & 1
        sent = total_of([pick(part, 1 - mine, axis) for part in parts]).astype(jnp.bfloat16)
        got = lax.ppermute(sent, "dp", [(i, i ^ (1 << bit)) for i in range(size)])
        parts = [pick(part, mine, axis) for part in parts] + [got]
        left.remove(bit)
    half = total_of(parts)
    other = lax.ppermute(half, "seq", SWAP)
    first = jnp.where(core == 0, half, other)
    second = jnp.where(core == 0, other, half)
    return jnp.concatenate([first, second], axis=0)


def shards(
    tokens,
    segments,
    query_weight,
    query_bias,
    key_weight,
    value_weight,
    value_bias,
    output_weight,
    output_bias,
    first_gain,
    first_shift,
    inner_weight,
    inner_bias,
    outer_weight,
    outer_bias,
    second_gain,
    second_shift,
    cotangent,
):
    rows, half, width = tokens.shape
    core = lax.axis_index("seq")
    size = lax.axis_size("dp")

    def whole_row(array):
        mine = pick(array, core, 0)
        other = lax.ppermute(pick(array, 1 - core, 0), "seq", SWAP)
        first = jnp.where(core == 0, mine, other)
        second = jnp.where(core == 0, other, mine)
        return jnp.concatenate([first, second], axis=0)

    def own_halves(array):
        array = array.reshape(2, half, width)
        mine = pick(array, core, 0)
        other = lax.ppermute(pick(array, 1 - core, 0), "seq", SWAP)
        first = jnp.where(core == 0, mine, other)
        second = jnp.where(core == 0, other, mine)
        return jnp.stack([first, second], axis=0)

    flattened = whole_row(tokens)
    grad_result = whole_row(cotangent).astype(jnp.float32)
    segment_row = pick(segments, core, 0)
    query = (dense(flattened, query_weight) + query_bias.astype(jnp.float32)).astype(jnp.bfloat16)
    key = dense(flattened, key_weight).astype(jnp.bfloat16)
    value = (dense(flattened, value_weight) + value_bias.astype(jnp.float32)).astype(jnp.bfloat16)
    context_rows, logsum = attend_forward((query, key, value, segment_row))
    attended = dense(context_rows, output_weight) + output_bias.astype(jnp.float32)
    first_sum = flattened.astype(jnp.float32) + attended
    first_norm, first_back = jax.vjp(
        layer_norm, first_sum, first_gain.astype(jnp.float32), first_shift.astype(jnp.float32)
    )
    norm_low = first_norm.astype(jnp.bfloat16)
    inner = dense(norm_low, inner_weight) + inner_bias.astype(jnp.float32)
    activation, gelu_back = jax.vjp(gelu_exact, inner)
    act_low = activation.astype(jnp.bfloat16)
    outer = dense(act_low, outer_weight) + outer_bias.astype(jnp.float32)
    second_sum = first_norm + outer
    result, second_back = jax.vjp(
        layer_norm, second_sum, second_gain.astype(jnp.float32), second_shift.astype(jnp.float32)
    )
    layer_out = own_halves(result.astype(jnp.bfloat16))
    grad_second, second_gain_term, second_shift_term = second_back(grad_result)
    grad_outer = grad_second.astype(jnp.bfloat16)
    outer_weight_term = dense(act_low.T, grad_outer)
    outer_weight_grad = scatter_sum(outer_weight_term, (0, 1, 2, 3))
    outer_bias_term = jnp.sum(grad_outer.astype(jnp.float32), axis=0)
    (grad_inner_full,) = gelu_back(dense(grad_outer, outer_weight.T))
    grad_inner = grad_inner_full.astype(jnp.bfloat16)
    inner_weight_term = dense(norm_low.T, grad_inner)
    inner_weight_grad = scatter_sum(inner_weight_term, (1, 2, 0, 3))
    inner_bias_term = jnp.sum(grad_inner.astype(jnp.float32), axis=0)
    grad_norm = grad_second + dense(grad_inner, inner_weight.T)
    grad_first, first_gain_term, first_shift_term = first_back(grad_norm)
    grad_attn = grad_first.astype(jnp.bfloat16)
    output_weight_term = dense(context_rows.T, grad_attn)
    output_bias_term = jnp.sum(grad_attn.astype(jnp.float32), axis=0)
    grad_context = dense(grad_attn, output_weight.T).astype(jnp.bfloat16)
    grad_query, grad_key, grad_value = attend_backward(
        (query, key, value, segment_row, grad_context, logsum)
    )
    query_weight_term = dense(flattened.T, grad_query)
    query_bias_term = jnp.sum(grad_query.astype(jnp.float32), axis=0)
    key_weight_term = dense(flattened.T, grad_key)
    value_weight_term = dense(flattened.T, grad_value)
    value_bias_term = jnp.sum(grad_value.astype(jnp.float32), axis=0)
    tokens_grad = (
        grad_first
        + dense(grad_query, query_weight.T)
        + dense(grad_key, key_weight.T)
        + dense(grad_value, value_weight.T)
    )
    tokens_grad = own_halves(tokens_grad.astype(jnp.bfloat16))
    vectors = [
        query_bias_term,
        value_bias_term,
        output_bias_term,
        first_gain_term,
        first_shift_term,
        inner_bias_term,
        outer_bias_term,
        second_gain_term,
        second_shift_term,
    ]
    packed = jnp.concatenate([v.reshape(size, -1) for v in vectors], axis=1)
    wide = packed.shape[1]
    pad = -wide % 256
    packed = jnp.pad(packed, ((0, 0), (0, pad))).reshape(size * 2, (wide + pad) // 2)
    packed_grad = scatter_sum(packed, (2, 0, 1, 3)).reshape(-1)
    vector_grads = []
    at = 0
    for v in vectors:
        step = v.shape[0] // size
        vector_grads.append(packed_grad[at : at + step])
        at += step
    output_weight_grad = scatter_sum(output_weight_term, (2, 0, 1, 3))
    query_weight_grad = scatter_sum(query_weight_term, (0, 1, 2, 3))
    key_weight_grad = scatter_sum(key_weight_term, (1, 2, 0, 3))
    value_weight_grad = scatter_sum(value_weight_term, (2, 0, 1, 3))
    (
        query_bias_grad,
        value_bias_grad,
        output_bias_grad,
        first_gain_grad,
        first_shift_grad,
        inner_bias_grad,
        outer_bias_grad,
        second_gain_grad,
        second_shift_grad,
    ) = vector_grads
    return (
        layer_out,
        tokens_grad,
        query_weight_grad,
        query_bias_grad,
        key_weight_grad,
        value_weight_grad,
        value_bias_grad,
        output_weight_grad,
        output_bias_grad,
        first_gain_grad,
        first_shift_grad,
        inner_weight_grad,
        inner_bias_grad,
        outer_weight_grad,
        outer_bias_grad,
        second_gain_grad,
        second_shift_grad,
    )


def solution(mesh):
    split = P("dp", "seq", None)
    return jax.shard_map(
        shards,
        mesh=mesh,
        in_specs=(split, P("dp", None)) + (P(),) * 15 + (split,),
        out_specs=(
            split,
            split,
            P("dp", None),
            P("dp"),
            P("dp", None),
            P("dp", None),
            P("dp"),
            P("dp", None),
            P("dp"),
            P("dp"),
            P("dp"),
            P("dp", None),
            P("dp"),
            P("dp", None),
            P("dp"),
            P("dp"),
            P("dp"),
        ),
        check_vma=False,
    )
```

```python
import jax
import jax.numpy as jnp
from jax import lax
from jax.experimental import pallas as pl
from jax.experimental.pallas import tpu as pltpu
from jax.sharding import PartitionSpec as P

HEAD_DIM = 64
DOCS = 8
MOST = 256
BLOCK = 128
WINDOW = 1 + 2 * MOST // BLOCK
LOWEST = -1e30
SWAP = [(0, 1), (1, 0)]


def layer_norm(summed, gain, shift):
    centre = summed - jnp.mean(summed, axis=-1, keepdims=True)
    spread = jnp.mean(centre * centre, axis=-1, keepdims=True)
    return centre * lax.rsqrt(spread + 1e-12) * gain + shift


def gelu_and_slope(inner):
    below = 0.5 + 0.5 * lax.erf(inner * 0.5**0.5)
    density = jnp.exp(-0.5 * inner * inner) * 0.3989422804014327
    return inner * below, below + inner * density


def dense(left, right):
    return jnp.dot(left, right, preferred_element_type=jnp.float32)


def key_windows(segments):
    length = segments.shape[0]
    blocks = segments.reshape(length // BLOCK, BLOCK)
    first = blocks[:, :1]
    last = jnp.minimum(blocks[:, -1:], DOCS - 2)
    before = jnp.sum((segments[None, :] < first).astype(jnp.int32), axis=1)
    upto = jnp.sum((segments[None, :] <= last).astype(jnp.int32), axis=1)
    low = before // BLOCK
    count = jnp.clip((upto + BLOCK - 1) // BLOCK - low, 0, WINDOW)
    count = jnp.where(first[:, 0] == DOCS - 1, 0, count)
    return jnp.minimum(low, length // BLOCK - count), count


def two_heads(pair):
    lane = lax.broadcasted_iota(jnp.int32, pair.shape, 1)
    zero = jnp.zeros_like(pair)
    return jnp.concatenate(
        [jnp.where(lane < HEAD_DIM, pair, zero), jnp.where(lane < HEAD_DIM, zero, pair)], axis=0
    )


def outer_dot(left, right):
    return lax.dot_general(
        left, right, (((1,), (1,)), ((), ())), preferred_element_type=jnp.float32
    )


def own_heads(both):
    return jnp.concatenate([both[:HEAD_DIM, :BLOCK], both[HEAD_DIM:, BLOCK:]], axis=0)


def pair_lanes(pair):
    return slice(pair * BLOCK, pair * BLOCK + BLOCK)


def forward_kernel(
    low_ref, count_ref, seg_row, seg_col, q_ref, k_ref, v_ref, ctx_ref, log_ref, turned
):
    at = pl.program_id(0)
    pairs = q_ref.shape[1] // BLOCK

    @pl.when(at == 0)
    def _():
        turned[...] = v_ref[...].T

    start = pl.multiple_of(low_ref[at] * BLOCK, BLOCK)
    row = seg_row[0]
    valid = row != DOCS - 1
    row = jnp.where(valid, row, -1)

    def work(count):
        window = pl.ds(start, count * BLOCK)
        allowed = seg_col[window, :] == row
        all_scores = []
        for pair in range(pairs):
            lanes = pair_lanes(pair)
            query = two_heads(q_ref[:, lanes] * jnp.bfloat16(0.125))
            all_scores.append(outer_dot(k_ref[window, lanes], query))
        logs = []
        for pair in range(pairs):
            lanes = pair_lanes(pair)
            weights = []
            inverse = []
            for head in range(2):
                own = jnp.where(allowed, all_scores[pair][:, pair_lanes(head)], LOWEST)
                top = jnp.max(own, axis=0, keepdims=True)
                exps = jnp.exp(own - top)
                total = jnp.sum(exps, axis=0, keepdims=True)
                weights.append(exps.astype(jnp.bfloat16))
                inverse.append(jnp.where(valid, 1.0 / total, 0.0))
                logs.append(jnp.where(valid, top + jnp.log(total), -LOWEST))
            both = dense(turned[lanes, window], jnp.concatenate(weights, axis=1))
            both = both * jnp.concatenate(inverse, axis=1)
            ctx_ref[:, lanes] = own_heads(both).T.astype(jnp.bfloat16)
        spare = log_ref.shape[0] - 2 * pairs
        if spare:
            logs.append(jnp.zeros((spare, BLOCK), jnp.float32))
        log_ref[...] = jnp.concatenate(logs, axis=0)

    @pl.when(count_ref[at] == 0)
    def _():
        ctx_ref[...] = jnp.zeros_like(ctx_ref)
        log_ref[...] = jnp.full_like(log_ref, -LOWEST)

    for count in range(1, WINDOW + 1):

        @pl.when(count_ref[at] == count)
        def _():
            work(count)


def backward_kernel(
    low_ref,
    count_ref,
    seg_row,
    seg_col,
    q_ref,
    k_ref,
    v_ref,
    g_ref,
    log_ref,
    dq_ref,
    dk_ref,
    dv_ref,
    turned,
    dk_sum,
    dv_sum,
):
    at = pl.program_id(0)
    pairs = q_ref.shape[1] // BLOCK

    @pl.when(at == 0)
    def _():
        turned[...] = k_ref[...].T
        dk_sum[...] = jnp.zeros_like(dk_sum)
        dv_sum[...] = jnp.zeros_like(dv_sum)

    start = pl.multiple_of(low_ref[at] * BLOCK, BLOCK)
    row = seg_row[0]
    row = jnp.where(row != DOCS - 1, row, -1)

    def work(count):
        window = pl.ds(start, count * BLOCK)
        allowed = seg_col[window, :] == row

        def products(pair):
            lanes = pair_lanes(pair)
            query = two_heads(q_ref[:, lanes] * jnp.bfloat16(0.125))
            grad = two_heads(g_ref[:, lanes])
            scores = outer_dot(k_ref[window, lanes], query)
            return query, grad, scores, outer_dot(v_ref[window, lanes], grad)

        def softmax(pair, query, grad, scores, grad_probs):
            probs_low = []
            grad_scores = []
            for head in range(2):
                cols = pair_lanes(head)
                log = log_ref[2 * pair + head : 2 * pair + head + 1, :]
                probs = jnp.exp(jnp.where(allowed, scores[:, cols], LOWEST) - log)
                own = grad_probs[:, cols]
                inner = jnp.sum(probs * own, axis=0, keepdims=True)
                probs_low.append(probs.astype(jnp.bfloat16))
                grad_scores.append((probs * (own - inner)).astype(jnp.bfloat16))
            joined = [jnp.concatenate(p, axis=1) for p in (probs_low, grad_scores)]
            return query, grad, *joined

        def results(pair, query, grad, probs_low, grad_scores):
            lanes = pair_lanes(pair)
            dv_sum[window, lanes] += dense(probs_low, grad)
            dk_sum[window, lanes] += dense(grad_scores, query)
            both = dense(turned[lanes, window], grad_scores)
            dq_ref[:, lanes] = (own_heads(both).T * 0.125).astype(jnp.bfloat16)

        ahead = products(0)
        behind = None
        for pair in range(pairs):
            now = ahead
            if pair + 1 < pairs:
                ahead = products(pair + 1)
            done = softmax(pair, *now)
            if pair > 0:
                results(pair - 1, *behind)
            behind = done
        results(pairs - 1, *behind)

    @pl.when(count_ref[at] == 0)
    def _():
        dq_ref[...] = jnp.zeros_like(dq_ref)

    for count in range(1, WINDOW + 1):

        @pl.when(count_ref[at] == count)
        def _():
            work(count)

    @pl.when(at == pl.num_programs(0) - 1)
    def _():
        dk_ref[...] = dk_sum[...].astype(jnp.bfloat16)
        dv_ref[...] = dv_sum[...].astype(jnp.bfloat16)


def attention_call(kernel, name, arrays, outputs, scratch, shape, flops):
    length, width = shape
    log_rows = width // HEAD_DIM + -(width // HEAD_DIM) % 8
    kinds = {
        "row": (pl.BlockSpec((1, 1, BLOCK), lambda i, *_: (i, 0, 0)), None),
        "col": (pl.BlockSpec((length, BLOCK), lambda i, *_: (0, 0)), None),
        "block": (
            pl.BlockSpec((BLOCK, width), lambda i, *_: (i, 0)),
            jax.ShapeDtypeStruct((length, width), jnp.bfloat16),
        ),
        "whole": (
            pl.BlockSpec((length, width), lambda i, *_: (0, 0)),
            jax.ShapeDtypeStruct((length, width), jnp.bfloat16),
        ),
        "logs": (
            pl.BlockSpec((log_rows, BLOCK), lambda i, *_: (0, i)),
            jax.ShapeDtypeStruct((log_rows, length), jnp.float32),
        ),
    }
    return pl.pallas_call(
        kernel,
        grid_spec=pltpu.PrefetchScalarGridSpec(
            num_scalar_prefetch=2,
            grid=(length // BLOCK,),
            in_specs=[kinds[k][0] for k in arrays],
            out_specs=[kinds[k][0] for k in outputs],
            scratch_shapes=scratch,
        ),
        out_shape=[kinds[k][1] for k in outputs],
        cost_estimate=pl.CostEstimate(
            flops=flops, bytes_accessed=2 * length * width * len(arrays), transcendentals=0
        ),
        name=name,
    )


def attend_forward(query, key, value, segments):
    length, width = query.shape
    call = attention_call(
        forward_kernel,
        "attend_forward",
        ["row", "col", "block", "whole", "whole"],
        ["block", "logs"],
        [pltpu.VMEM((width, length), jnp.bfloat16)],
        (length, width),
        16 * length * width * BLOCK * WINDOW,
    )
    return call(*segments, query, key, value)


def attend_backward(query, key, value, segments, grad_context, logs):
    length, width = query.shape
    call = attention_call(
        backward_kernel,
        "attend_backward",
        ["row", "col", "block", "whole", "whole", "block", "logs"],
        ["block", "whole", "whole"],
        [pltpu.VMEM((width, length), jnp.bfloat16)] + [pltpu.VMEM((length, width), jnp.float32)] * 2,
        (length, width),
        32 * length * width * BLOCK * WINDOW,
    )
    return call(*segments, query, key, value, grad_context, logs)


def pick(array, index, axis):
    return lax.dynamic_index_in_dim(array, index, axis, keepdims=False)


def total_of(parts):
    result = parts[0].astype(jnp.float32)
    for part in parts[1:]:
        result = result + part.astype(jnp.float32)
    return result


def scatter_sum(term, order):
    size = lax.axis_size("dp")
    me = lax.axis_index("dp")
    core = lax.axis_index("seq")
    bits = size.bit_length() - 1
    rows, columns = term.shape
    own = rows // size // 2
    term = term.reshape((2,) * bits + (2, own, columns))
    sent = pick(term, 1 - core, bits).astype(jnp.bfloat16)
    parts = [pick(term, core, bits), lax.ppermute(sent, "seq", SWAP)]
    left = list(range(bits - 1, -1, -1))
    for bit in [b for b in order if b < bits] + [b for b in range(bits) if b not in order]:
        axis = left.index(bit)
        mine = (me >> bit) & 1
        sent = total_of([pick(part, 1 - mine, axis) for part in parts]).astype(jnp.bfloat16)
        got = lax.ppermute(sent, "dp", [(i, i ^ (1 << bit)) for i in range(size)])
        parts = [pick(part, mine, axis) for part in parts] + [got]
        left.remove(bit)
    half = total_of(parts)
    other = lax.ppermute(half, "seq", SWAP)
    first = jnp.where(core == 0, half, other)
    second = jnp.where(core == 0, other, half)
    return jnp.concatenate([first, second], axis=0)


def shards(
    tokens,
    segments,
    query_weight,
    query_bias,
    key_weight,
    value_weight,
    value_bias,
    output_weight,
    output_bias,
    first_gain,
    first_shift,
    inner_weight,
    inner_bias,
    outer_weight,
    outer_bias,
    second_gain,
    second_shift,
    cotangent,
):
    rows, half, width = tokens.shape
    core = lax.axis_index("seq")
    size = lax.axis_size("dp")

    def whole_row(array):
        mine = pick(array, core, 0)
        other = lax.ppermute(pick(array, 1 - core, 0), "seq", SWAP)
        first = jnp.where(core == 0, mine, other)
        second = jnp.where(core == 0, other, mine)
        return jnp.concatenate([first, second], axis=0)

    def own_halves(array):
        array = array.reshape(2, half, width)
        mine = pick(array, core, 0)
        other = lax.ppermute(pick(array, 1 - core, 0), "seq", SWAP)
        first = jnp.where(core == 0, mine, other)
        second = jnp.where(core == 0, other, mine)
        return jnp.stack([first, second], axis=0)

    flattened = whole_row(tokens)
    grad_result = whole_row(cotangent).astype(jnp.float32)
    segment_row = pick(segments, core, 0)
    query = (dense(flattened, query_weight) + query_bias.astype(jnp.float32)).astype(jnp.bfloat16)
    key = dense(flattened, key_weight).astype(jnp.bfloat16)
    value = (dense(flattened, value_weight) + value_bias.astype(jnp.float32)).astype(jnp.bfloat16)
    length = 2 * half
    low, count = key_windows(segment_row)
    place = (
        low,
        count,
        segment_row.reshape(length // BLOCK, 1, BLOCK),
        jnp.broadcast_to(segment_row[:, None], (length, BLOCK)),
    )
    context_rows, logsum = attend_forward(query, key, value, place)
    attended = dense(context_rows, output_weight) + output_bias.astype(jnp.float32)
    first_sum = flattened.astype(jnp.float32) + attended
    first_norm, first_back = jax.vjp(
        layer_norm, first_sum, first_gain.astype(jnp.float32), first_shift.astype(jnp.float32)
    )
    norm_low = first_norm.astype(jnp.bfloat16)
    inner = dense(norm_low, inner_weight) + inner_bias.astype(jnp.float32)
    activation, slope = gelu_and_slope(inner)
    act_low = activation.astype(jnp.bfloat16)
    slope = slope.astype(jnp.bfloat16)
    outer = dense(act_low, outer_weight) + outer_bias.astype(jnp.float32)
    second_sum = first_norm + outer
    result, second_back = jax.vjp(
        layer_norm, second_sum, second_gain.astype(jnp.float32), second_shift.astype(jnp.float32)
    )
    layer_out = own_halves(result.astype(jnp.bfloat16))
    grad_second, second_gain_term, second_shift_term = second_back(grad_result)
    grad_outer = grad_second.astype(jnp.bfloat16)
    outer_weight_term = dense(act_low.T, grad_outer)
    outer_weight_grad = scatter_sum(outer_weight_term, (0, 1, 2, 3))
    outer_bias_term = jnp.sum(grad_outer.astype(jnp.float32), axis=0)
    grad_inner = dense(grad_outer, outer_weight.T) * slope.astype(jnp.float32)
    grad_inner = grad_inner.astype(jnp.bfloat16)
    inner_weight_term = dense(norm_low.T, grad_inner)
    inner_weight_grad = scatter_sum(inner_weight_term, (1, 2, 0, 3))
    inner_bias_term = jnp.sum(grad_inner.astype(jnp.float32), axis=0)
    grad_norm = grad_second + dense(grad_inner, inner_weight.T)
    grad_first, first_gain_term, first_shift_term = first_back(grad_norm)
    grad_attn = grad_first.astype(jnp.bfloat16)
    output_weight_term = dense(context_rows.T, grad_attn)
    output_bias_term = jnp.sum(grad_attn.astype(jnp.float32), axis=0)
    grad_context = dense(grad_attn, output_weight.T).astype(jnp.bfloat16)
    grad_query, grad_key, grad_value = attend_backward(
        query, key, value, place, grad_context, logsum
    )
    query_weight_term = dense(flattened.T, grad_query)
    query_bias_term = jnp.sum(grad_query.astype(jnp.float32), axis=0)
    key_weight_term = dense(flattened.T, grad_key)
    value_weight_term = dense(flattened.T, grad_value)
    value_bias_term = jnp.sum(grad_value.astype(jnp.float32), axis=0)
    tokens_grad = (
        grad_first
        + dense(grad_query, query_weight.T)
        + dense(grad_key, key_weight.T)
        + dense(grad_value, value_weight.T)
    )
    tokens_grad = own_halves(tokens_grad.astype(jnp.bfloat16))
    vectors = [
        query_bias_term,
        value_bias_term,
        output_bias_term,
        first_gain_term,
        first_shift_term,
        inner_bias_term,
        outer_bias_term,
        second_gain_term,
        second_shift_term,
    ]
    packed = jnp.concatenate([v.reshape(size, -1) for v in vectors], axis=1)
    wide = packed.shape[1]
    pad = -wide % 256
    packed = jnp.pad(packed, ((0, 0), (0, pad))).reshape(size * 2, (wide + pad) // 2)
    packed_grad = scatter_sum(packed, (2, 0, 1, 3)).reshape(-1)
    vector_grads = []
    at = 0
    for v in vectors:
        step = v.shape[0] // size
        vector_grads.append(packed_grad[at : at + step])
        at += step
    output_weight_grad = scatter_sum(output_weight_term, (2, 0, 1, 3))
    query_weight_grad = scatter_sum(query_weight_term, (0, 1, 2, 3))
    key_weight_grad = scatter_sum(key_weight_term, (1, 2, 0, 3))
    value_weight_grad = scatter_sum(value_weight_term, (2, 0, 1, 3))
    (
        query_bias_grad,
        value_bias_grad,
        output_bias_grad,
        first_gain_grad,
        first_shift_grad,
        inner_bias_grad,
        outer_bias_grad,
        second_gain_grad,
        second_shift_grad,
    ) = vector_grads
    return (
        layer_out,
        tokens_grad,
        query_weight_grad,
        query_bias_grad,
        key_weight_grad,
        value_weight_grad,
        value_bias_grad,
        output_weight_grad,
        output_bias_grad,
        first_gain_grad,
        first_shift_grad,
        inner_weight_grad,
        inner_bias_grad,
        outer_weight_grad,
        outer_bias_grad,
        second_gain_grad,
        second_shift_grad,
    )


def solution(mesh):
    split = P("dp", "seq", None)
    return jax.shard_map(
        shards,
        mesh=mesh,
        in_specs=(split, P("dp", None)) + (P(),) * 15 + (split,),
        out_specs=(
            split,
            split,
            P("dp", None),
            P("dp"),
            P("dp", None),
            P("dp", None),
            P("dp"),
            P("dp", None),
            P("dp"),
            P("dp"),
            P("dp"),
            P("dp", None),
            P("dp"),
            P("dp", None),
            P("dp"),
            P("dp"),
            P("dp"),
        ),
        check_vma=False,
    )
```

```python
import jax
import jax.numpy as jnp
from jax import lax
from jax.experimental import pallas as pl
from jax.experimental.pallas import tpu as pltpu
from jax.sharding import PartitionSpec as P

HEAD_DIM = 64
DOCS = 8
MOST = 256
BLOCK = 128
WINDOW = 1 + 2 * MOST // BLOCK
LOWEST = -1e30
ROWS = 256
TILE = 512
SWAP = [(0, 1), (1, 0)]


def dense(left, right):
    return jnp.dot(left, right, preferred_element_type=jnp.float32)


def key_windows(segments):
    length = segments.shape[0]
    blocks = segments.reshape(length // BLOCK, BLOCK)
    first = blocks[:, :1]
    last = jnp.minimum(blocks[:, -1:], DOCS - 2)
    before = jnp.sum((segments[None, :] < first).astype(jnp.int32), axis=1)
    upto = jnp.sum((segments[None, :] <= last).astype(jnp.int32), axis=1)
    low = before // BLOCK
    count = jnp.clip((upto + BLOCK - 1) // BLOCK - low, 0, WINDOW)
    count = jnp.where(first[:, 0] == DOCS - 1, 0, count)
    return jnp.minimum(low, length // BLOCK - count), count


def two_heads(pair):
    lane = lax.broadcasted_iota(jnp.int32, pair.shape, 1)
    zero = jnp.zeros_like(pair)
    return jnp.concatenate(
        [jnp.where(lane < HEAD_DIM, pair, zero), jnp.where(lane < HEAD_DIM, zero, pair)], axis=0
    )


def outer_dot(left, right):
    return lax.dot_general(
        left, right, (((1,), (1,)), ((), ())), preferred_element_type=jnp.float32
    )


def own_heads(both):
    return jnp.concatenate([both[:HEAD_DIM, :BLOCK], both[HEAD_DIM:, BLOCK:]], axis=0)


def pair_lanes(pair):
    return slice(pair * BLOCK, pair * BLOCK + BLOCK)


def forward_kernel(
    low_ref, count_ref, seg_row, seg_col, q_ref, k_ref, v_ref, ctx_ref, log_ref, turned
):
    at = pl.program_id(0)
    pairs = q_ref.shape[1] // BLOCK

    @pl.when(at == 0)
    def _():
        turned[...] = v_ref[...].T

    start = pl.multiple_of(low_ref[at] * BLOCK, BLOCK)
    row = seg_row[0]
    valid = row != DOCS - 1
    row = jnp.where(valid, row, -1)

    def work(count):
        window = pl.ds(start, count * BLOCK)
        allowed = seg_col[window, :] == row
        all_scores = []
        for pair in range(pairs):
            lanes = pair_lanes(pair)
            query = two_heads(q_ref[:, lanes] * jnp.bfloat16(0.125))
            all_scores.append(outer_dot(k_ref[window, lanes], query))
        logs = []
        for pair in range(pairs):
            lanes = pair_lanes(pair)
            weights = []
            inverse = []
            for head in range(2):
                own = jnp.where(allowed, all_scores[pair][:, pair_lanes(head)], LOWEST)
                top = jnp.max(own, axis=0, keepdims=True)
                exps = jnp.exp(own - top)
                total = jnp.sum(exps, axis=0, keepdims=True)
                weights.append(exps.astype(jnp.bfloat16))
                inverse.append(jnp.where(valid, 1.0 / total, 0.0))
                logs.append(jnp.where(valid, top + jnp.log(total), -LOWEST))
            both = dense(turned[lanes, window], jnp.concatenate(weights, axis=1))
            both = both * jnp.concatenate(inverse, axis=1)
            ctx_ref[:, lanes] = own_heads(both).T.astype(jnp.bfloat16)
        spare = log_ref.shape[0] - 2 * pairs
        if spare:
            logs.append(jnp.zeros((spare, BLOCK), jnp.float32))
        log_ref[...] = jnp.concatenate(logs, axis=0)

    @pl.when(count_ref[at] == 0)
    def _():
        ctx_ref[...] = jnp.zeros_like(ctx_ref)
        log_ref[...] = jnp.full_like(log_ref, -LOWEST)

    for count in range(1, WINDOW + 1):

        @pl.when(count_ref[at] == count)
        def _():
            work(count)


def backward_kernel(
    low_ref,
    count_ref,
    seg_row,
    seg_col,
    q_ref,
    k_ref,
    v_ref,
    g_ref,
    log_ref,
    dq_ref,
    dk_ref,
    dv_ref,
    sum_ref,
    turned,
    dk_sum,
    dv_sum,
):
    at = pl.program_id(0)
    pairs = q_ref.shape[1] // BLOCK

    @pl.when(at == 0)
    def _():
        turned[...] = k_ref[...].T
        dk_sum[...] = jnp.zeros_like(dk_sum)
        dv_sum[...] = jnp.zeros_like(dv_sum)
        sum_ref[...] = jnp.zeros_like(sum_ref)

    start = pl.multiple_of(low_ref[at] * BLOCK, BLOCK)
    row = seg_row[0]
    row = jnp.where(row != DOCS - 1, row, -1)

    def work(count):
        window = pl.ds(start, count * BLOCK)
        allowed = seg_col[window, :] == row

        def products(pair):
            lanes = pair_lanes(pair)
            query = two_heads(q_ref[:, lanes] * jnp.bfloat16(0.125))
            grad = two_heads(g_ref[:, lanes])
            scores = outer_dot(k_ref[window, lanes], query)
            return query, grad, scores, outer_dot(v_ref[window, lanes], grad)

        def softmax(pair, query, grad, scores, grad_probs):
            probs_low = []
            grad_scores = []
            for head in range(2):
                cols = pair_lanes(head)
                log = log_ref[2 * pair + head : 2 * pair + head + 1, :]
                probs = jnp.exp(jnp.where(allowed, scores[:, cols], LOWEST) - log)
                own = grad_probs[:, cols]
                inner = jnp.sum(probs * own, axis=0, keepdims=True)
                probs_low.append(probs.astype(jnp.bfloat16))
                grad_scores.append((probs * (own - inner)).astype(jnp.bfloat16))
            joined = [jnp.concatenate(p, axis=1) for p in (probs_low, grad_scores)]
            return query, grad, *joined

        def results(pair, query, grad, probs_low, grad_scores):
            lanes = pair_lanes(pair)
            dv_sum[window, lanes] += dense(probs_low, grad)
            dk_sum[window, lanes] += dense(grad_scores, query)
            both = dense(turned[lanes, window], grad_scores)
            query_grad = (own_heads(both).T * 0.125).astype(jnp.bfloat16)
            dq_ref[:, lanes] = query_grad
            sum_ref[0:1, lanes] += column_sum(query_grad)

        ahead = products(0)
        behind = None
        for pair in range(pairs):
            now = ahead
            if pair + 1 < pairs:
                ahead = products(pair + 1)
            done = softmax(pair, *now)
            if pair > 0:
                results(pair - 1, *behind)
            behind = done
        results(pairs - 1, *behind)

    @pl.when(count_ref[at] == 0)
    def _():
        dq_ref[...] = jnp.zeros_like(dq_ref)

    for count in range(1, WINDOW + 1):

        @pl.when(count_ref[at] == count)
        def _():
            work(count)

    @pl.when(at == pl.num_programs(0) - 1)
    def _():
        dk_ref[...] = dk_sum[...].astype(jnp.bfloat16)
        value_grad = dv_sum[...].astype(jnp.bfloat16)
        dv_ref[...] = value_grad
        sum_ref[1:2, :] = column_sum(value_grad)


def attention_call(kernel, name, arrays, outputs, scratch, shape, flops):
    length, width = shape
    log_rows = width // HEAD_DIM + -(width // HEAD_DIM) % 8
    kinds = {
        "row": (pl.BlockSpec((1, 1, BLOCK), lambda i, *_: (i, 0, 0)), None),
        "col": (pl.BlockSpec((length, BLOCK), lambda i, *_: (0, 0)), None),
        "block": (
            pl.BlockSpec((BLOCK, width), lambda i, *_: (i, 0)),
            jax.ShapeDtypeStruct((length, width), jnp.bfloat16),
        ),
        "whole": (
            pl.BlockSpec((length, width), lambda i, *_: (0, 0)),
            jax.ShapeDtypeStruct((length, width), jnp.bfloat16),
        ),
        "sums": (
            pl.BlockSpec((8, width), lambda i, *_: (0, 0)),
            jax.ShapeDtypeStruct((8, width), jnp.float32),
        ),
        "logs": (
            pl.BlockSpec((log_rows, BLOCK), lambda i, *_: (0, i)),
            jax.ShapeDtypeStruct((log_rows, length), jnp.float32),
        ),
    }
    return pl.pallas_call(
        kernel,
        grid_spec=pltpu.PrefetchScalarGridSpec(
            num_scalar_prefetch=2,
            grid=(length // BLOCK,),
            in_specs=[kinds[k][0] for k in arrays],
            out_specs=[kinds[k][0] for k in outputs],
            scratch_shapes=scratch,
        ),
        out_shape=[kinds[k][1] for k in outputs],
        cost_estimate=pl.CostEstimate(
            flops=flops, bytes_accessed=2 * length * width * len(arrays), transcendentals=0
        ),
        name=name,
    )


def attend_forward(query, key, value, segments):
    length, width = query.shape
    call = attention_call(
        forward_kernel,
        "attend_forward",
        ["row", "col", "block", "whole", "whole"],
        ["block", "logs"],
        [pltpu.VMEM((width, length), jnp.bfloat16)],
        (length, width),
        16 * length * width * BLOCK * WINDOW,
    )
    return call(*segments, query, key, value)


def attend_backward(query, key, value, segments, grad_context, logs):
    length, width = query.shape
    call = attention_call(
        backward_kernel,
        "attend_backward",
        ["row", "col", "block", "whole", "whole", "block", "logs"],
        ["block", "whole", "whole", "sums"],
        [pltpu.VMEM((width, length), jnp.bfloat16)] + [pltpu.VMEM((length, width), jnp.float32)] * 2,
        (length, width),
        32 * length * width * BLOCK * WINDOW,
    )
    return call(*segments, query, key, value, grad_context, logs)


def normalize(summed):
    centre = summed - jnp.mean(summed, axis=-1, keepdims=True)
    scale = lax.rsqrt(jnp.mean(centre * centre, axis=-1, keepdims=True) + 1e-12)
    return centre * scale, scale


def norm_grad(grad, normal, scale):
    mean = jnp.mean(grad, axis=-1, keepdims=True)
    along = jnp.mean(grad * normal, axis=-1, keepdims=True)
    return scale * (grad - mean - normal * along)


def column_sum(array):
    return jnp.sum(array.astype(jnp.float32), axis=0, keepdims=True)


def middle_kernel(core_ref, x_ref, ctx_ref, dy_ref, vec_ref, bias_ref, wo_ref, w1_ref, w2_ref,
                  out_ref, act_ref, low_ref, gom_ref, goo_ref, gim_ref, gio_ref, ga_ref, gc_ref,
                  sum_ref, hid_ref, slope):
    at = pl.program_id(0)
    core = core_ref[0]
    width = x_ref.shape[1]
    hidden = w1_ref.shape[1]
    tiles = [slice(i, i + TILE) for i in range(0, hidden, TILE)]
    out_bias, gain1, shift1, outer_bias, gain2, shift2 = [
        vec_ref[i : i + 1, :].astype(jnp.float32) for i in range(6)
    ]

    @pl.when(at == 0)
    def _():
        sum_ref[...] = jnp.zeros_like(sum_ref)
        hid_ref[...] = jnp.zeros_like(hid_ref)

    first_sum = x_ref[...].astype(jnp.float32) + (dense(ctx_ref[...], wo_ref[...]) + out_bias)
    normal1, scale1 = normalize(first_sum)
    first_norm = normal1 * gain1 + shift1
    low = first_norm.astype(jnp.bfloat16)
    low_ref[...] = low

    def inner_of(tile):
        return dense(low, w1_ref[:, tile]) + bias_ref[:, tile].astype(jnp.float32)

    def gelu(tile, inner):
        below = 0.5 + 0.5 * lax.erf(inner * 0.5**0.5)
        density = jnp.exp(-0.5 * inner * inner) * 0.3989422804014327
        slope[:, tile] = (below + inner * density).astype(jnp.bfloat16)
        act = (inner * below).astype(jnp.bfloat16)
        act_ref[:, tile] = act
        return act

    outer = outer_bias
    ahead = inner_of(tiles[0])
    for i, tile in enumerate(tiles):
        now = ahead
        if i + 1 < len(tiles):
            ahead = inner_of(tiles[i + 1])
        outer = outer + dense(gelu(tile, now), w2_ref[tile, :])
    normal2, scale2 = normalize(first_norm + outer)
    out_ref[...] = (normal2 * gain2 + shift2).astype(jnp.bfloat16)
    dy = dy_ref[...].astype(jnp.float32)
    sum_ref[0:1, :] += column_sum(dy * normal2)
    sum_ref[1:2, :] += column_sum(dy)
    grad_second = norm_grad(dy * gain2, normal2, scale2)
    grad_outer = grad_second.astype(jnp.bfloat16)
    sum_ref[2:3, :] += column_sum(grad_outer)
    left, right = grad_outer[:, : width // 2], grad_outer[:, width // 2 :]
    gom_ref[...] = jnp.where(core == 0, left, right)
    goo_ref[...] = jnp.where(core == 0, right, left)

    grad_norm = grad_second
    ahead = outer_dot(grad_outer, w2_ref[tiles[0], :])
    for i, tile in enumerate(tiles):
        now = ahead
        if i + 1 < len(tiles):
            ahead = outer_dot(grad_outer, w2_ref[tiles[i + 1], :])
        grad = (now * slope[:, tile].astype(jnp.float32)).astype(jnp.bfloat16)
        hid_ref[:, tile] += column_sum(grad)
        slope[:, tile] = grad
        grad_norm = grad_norm + outer_dot(grad, w1_ref[:, tile])
    for index, mine, other in ((0, gim_ref, gio_ref), (1, gio_ref, gim_ref)):

        @pl.when(core == index)
        def _():
            mine[...] = slope[:, : hidden // 2]
            other[...] = slope[:, hidden // 2 :]

    sum_ref[3:4, :] += column_sum(grad_norm * normal1)
    sum_ref[4:5, :] += column_sum(grad_norm)
    grad_attn = norm_grad(grad_norm * gain1, normal1, scale1).astype(jnp.bfloat16)
    sum_ref[5:6, :] += column_sum(grad_attn)
    ga_ref[...] = grad_attn
    gc_ref[...] = outer_dot(grad_attn, wo_ref[...]).astype(jnp.bfloat16)


def middle(core, x, ctx, dy, vec, bias, wo, w1, w2):
    length, width = x.shape
    hidden = w1.shape[1]

    def rows(columns):
        return pl.BlockSpec((ROWS, columns), lambda i, *_: (i, 0))

    def whole(array):
        return pl.BlockSpec(array.shape, lambda i, *_: (0, 0), pipeline_mode=pl.Buffered(1))

    def out(columns):
        return jax.ShapeDtypeStruct((length, columns), jnp.bfloat16)

    outs = [width, hidden, width, width // 2, width // 2, hidden // 2, hidden // 2, width, width]
    return pl.pallas_call(
        middle_kernel,
        grid_spec=pltpu.PrefetchScalarGridSpec(
            num_scalar_prefetch=1,
            grid=(length // ROWS,),
            in_specs=[rows(width)] * 3 + [whole(a) for a in (vec, bias, wo, w1, w2)],
            out_specs=[rows(c) for c in outs] + [pl.BlockSpec((8, width), lambda i, *_: (0, 0)), pl.BlockSpec((1, hidden), lambda i, *_: (0, 0))],
            scratch_shapes=[pltpu.VMEM((ROWS, hidden), jnp.bfloat16)],
        ),
        out_shape=[out(c) for c in outs] + [jax.ShapeDtypeStruct((8, width), jnp.float32), jax.ShapeDtypeStruct((1, hidden), jnp.float32)],
        cost_estimate=pl.CostEstimate(
            flops=4 * length * width * (width + 2 * hidden),
            bytes_accessed=2 * length * (8 * width + 3 * hidden),
            transcendentals=0,
        ),
        name="middle",
    )(core, x, ctx, dy, vec, bias, wo, w1, w2)


def pick(array, index, axis):
    return lax.dynamic_index_in_dim(array, index, axis, keepdims=False)


def total_of(parts):
    result = parts[0].astype(jnp.float32)
    for part in parts[1:]:
        result = result + part.astype(jnp.float32)
    return result


def tie(*arrays):
    return lax.optimization_barrier(arrays)


def swap(array):
    return lax.ppermute(array, "seq", SWAP)


class Halving:
    def __init__(self, parts, order):
        self.size = lax.axis_size("dp")
        self.me = lax.axis_index("dp")
        bits = self.size.bit_length() - 1
        self.left = list(range(bits - 1, -1, -1))
        self.order = [b for b in order if b < bits] + [b for b in range(bits) if b not in order]
        rows, columns = parts[0].shape
        self.parts = [p.reshape((2,) * bits + (rows // self.size, columns)) for p in parts]
        self.got = None

    def send(self):
        if not self.order:
            return
        bit = self.order.pop(0)
        axis = self.left.index(bit)
        mine = (self.me >> bit) & 1
        sent = total_of([pick(part, 1 - mine, axis) for part in self.parts]).astype(jnp.bfloat16)
        pairs = [(i, i ^ (1 << bit)) for i in range(self.size)]
        self.got = lax.ppermute(sent, "dp", pairs)
        self.parts = [pick(part, mine, axis) for part in self.parts]
        self.left.remove(bit)

    def take(self):
        if self.got is not None:
            self.parts = self.parts + [self.got]
            self.got = None

    def finish(self):
        self.take()
        while self.order:
            self.send()
            self.take()
        return total_of(self.parts)


class Doubling:
    def __init__(self, array):
        self.size = lax.axis_size("dp")
        self.order = list(range(self.size.bit_length() - 1))
        self.total = array
        self.got = None

    def send(self):
        if not self.order:
            return
        bit = self.order.pop(0)
        pairs = [(i, i ^ (1 << bit)) for i in range(self.size)]
        self.sent = self.total.astype(jnp.bfloat16)
        self.got = lax.ppermute(self.sent, "dp", pairs)

    def take(self):
        if self.got is not None:
            self.total = total_of([self.sent, self.got])
            self.got = None

    def finish(self):
        self.take()
        while self.order:
            self.send()
            self.take()
        return self.total


def advance(works, *arrays):
    waiting = [w for w in works if w.got is not None]
    out = tie(*[w.got for w in waiting], *arrays)
    for work, got in zip(waiting, out):
        work.got = got
        work.take()
    for work in works:
        work.send()
    return out[len(waiting) :]


def shards(
    tokens,
    segments,
    query_weight,
    query_bias,
    key_weight,
    value_weight,
    value_bias,
    output_weight,
    output_bias,
    first_gain,
    first_shift,
    inner_weight,
    inner_bias,
    outer_weight,
    outer_bias,
    second_gain,
    second_shift,
    cotangent,
):
    rows, half, width = tokens.shape
    core = lax.axis_index("seq")
    size = lax.axis_size("dp")

    def whole_row(array):
        mine = pick(array, core, 0)
        other = lax.ppermute(pick(array, 1 - core, 0), "seq", SWAP)
        first = jnp.where(core == 0, mine, other)
        second = jnp.where(core == 0, other, mine)
        return jnp.concatenate([first, second], axis=0)

    def own_halves(array):
        array = array.reshape(2, half, width)
        mine = pick(array, core, 0)
        other = lax.ppermute(pick(array, 1 - core, 0), "seq", SWAP)
        first = jnp.where(core == 0, mine, other)
        second = jnp.where(core == 0, other, mine)
        return jnp.stack([first, second], axis=0)

    flattened = whole_row(tokens)
    grad_result = whole_row(cotangent)
    segment_row = pick(segments, core, 0)
    query = (dense(flattened, query_weight) + query_bias.astype(jnp.float32)).astype(jnp.bfloat16)
    key = dense(flattened, key_weight).astype(jnp.bfloat16)
    value = (dense(flattened, value_weight) + value_bias.astype(jnp.float32)).astype(jnp.bfloat16)
    length = 2 * half
    place = (
        *key_windows(segment_row),
        segment_row.reshape(length // BLOCK, 1, BLOCK),
        jnp.broadcast_to(segment_row[:, None], (length, BLOCK)),
    )
    context_rows, logsum = attend_forward(query, key, value, place)
    scales = jnp.stack(
        [output_bias, first_gain, first_shift, outer_bias, second_gain, second_shift]
    )
    (
        result,
        act_low,
        norm_low,
        outer_mine,
        outer_other,
        inner_mine,
        inner_other,
        grad_attn,
        grad_context,
        middle_sums,
        inner_bias_term,
    ) = middle(
        core.astype(jnp.int32).reshape(1),
        flattened,
        context_rows,
        grad_result,
        scales,
        inner_bias.reshape(1, -1),
        output_weight,
        inner_weight,
        outer_weight,
    )
    layer_out = own_halves(result)

    def part_of(array, index):
        columns = array.shape[1] // 2
        return lax.dynamic_slice_in_dim(array, index * columns, columns, axis=1)

    def send_part(left, right):
        return dense(left.T, right).astype(jnp.bfloat16)

    outer_sent, outer_mine, inner_other = tie(
        send_part(act_low, outer_other), outer_mine, inner_other
    )
    outer_got = swap(outer_sent)
    inner_sent, outer_mine = tie(send_part(norm_low, inner_other), outer_mine)
    inner_got = swap(inner_sent)
    outer_kept = dense(act_low.T, outer_mine)
    outer_got, outer_kept, inner_mine = tie(outer_got, outer_kept, inner_mine)
    outer_work = Halving([outer_kept, outer_got], (0, 1, 2, 3))
    outer_work.send()
    inner_kept = dense(norm_low.T, inner_mine)
    inner_got, inner_kept, grad_attn = tie(inner_got, inner_kept, grad_attn)
    inner_work = Halving([inner_kept, inner_got], (2, 0, 1, 3))
    inner_work.send()
    output_sent = send_part(context_rows, part_of(grad_attn, 1 - core))
    output_kept = dense(context_rows.T, part_of(grad_attn, core))
    output_sent, output_kept, grad_context = tie(output_sent, output_kept, grad_context)
    grad_query, grad_key, grad_value, attention_sums = attend_backward(
        query, key, value, place, grad_context, logsum
    )
    three = (grad_query, grad_key, grad_value)
    others = [send_part(flattened, part_of(g, 1 - core)) for g in three]
    others = jnp.concatenate(others + [output_sent], axis=1)
    small = jnp.concatenate(
        [attention_sums[:2], middle_sums[:6], inner_bias_term.reshape(-1, width)], axis=0
    )
    small = jnp.pad(small, ((0, -small.shape[0] % 16), (0, 0)))
    small_low = small.astype(jnp.bfloat16)
    others, small_low, *three = advance([outer_work, inner_work], others, small_low, *three)
    others = swap(others)
    small_other = swap(small_low)
    kept = [dense(flattened.T, part_of(g, core)) for g in three] + [output_kept]
    kept = jnp.concatenate(kept, axis=1)
    others, small_other, kept, *three = tie(others, small_other, kept, *three)
    columns = 2 * width // 3
    small_work = Doubling(total_of([small_low, small_other]))
    chunk_works = []
    for index, order in enumerate([(0, 1, 2, 3), (1, 2, 0, 3), (2, 0, 1, 3)]):
        take = slice(index * columns, index * columns + columns)
        work = Halving([kept[:, take], others[:, take]], order)
        work.send()
        chunk_works.append(work)
    small_work.send()
    tokens_grad = grad_attn.astype(jnp.float32)
    for grad, weight in zip(three, (query_weight, key_weight, value_weight)):
        tokens_grad = tokens_grad + dense(grad, weight.T)
    (tokens_grad,) = advance(
        [outer_work, inner_work] + chunk_works + [small_work], tokens_grad.astype(jnp.bfloat16)
    )
    tokens_grad = own_halves(tokens_grad)

    def both_halves(half):
        other = swap(half)
        first = jnp.where(core == 0, half, other)
        second = jnp.where(core == 0, other, half)
        return jnp.concatenate([first, second], axis=1)

    for _ in range(size.bit_length()):
        for work in [outer_work, inner_work] + chunk_works + [small_work]:
            work.take()
            work.send()
    outer_weight_grad = both_halves(outer_work.finish())
    inner_weight_grad = both_halves(inner_work.finish())
    mine = jnp.concatenate([work.finish() for work in chunk_works], axis=1)
    other = swap(mine)
    first = jnp.where(core == 0, mine, other)
    second = jnp.where(core == 0, other, mine)
    query_weight_grad, key_weight_grad, value_weight_grad, output_weight_grad = [
        jnp.concatenate([h[:, i * (width // 2) : (i + 1) * (width // 2)] for h in (first, second)], axis=1)
        for i in range(4)
    ]
    sums = small_work.finish()
    own = width // size
    me = lax.axis_index("dp")
    own_sums = lax.dynamic_slice_in_dim(sums, me * own, own, axis=1)
    (
        query_bias_grad,
        value_bias_grad,
        second_gain_grad,
        second_shift_grad,
        outer_bias_grad,
        first_gain_grad,
        first_shift_grad,
        output_bias_grad,
    ) = [own_sums[i] for i in range(8)]
    wide = inner_bias.shape[0] // size
    per_row = width // wide
    inner_bias_grad = lax.dynamic_slice(
        sums, (8 + me // per_row, me % per_row * wide), (1, wide)
    ).reshape(-1)
    return (
        layer_out,
        tokens_grad,
        query_weight_grad,
        query_bias_grad,
        key_weight_grad,
        value_weight_grad,
        value_bias_grad,
        output_weight_grad,
        output_bias_grad,
        first_gain_grad,
        first_shift_grad,
        inner_weight_grad,
        inner_bias_grad,
        outer_weight_grad,
        outer_bias_grad,
        second_gain_grad,
        second_shift_grad,
    )


def solution(mesh):
    split = P("dp", "seq", None)
    return jax.shard_map(
        shards,
        mesh=mesh,
        in_specs=(split, P("dp", None)) + (P(),) * 15 + (split,),
        out_specs=(
            split,
            split,
            P("dp", None),
            P("dp"),
            P("dp", None),
            P("dp", None),
            P("dp"),
            P("dp", None),
            P("dp"),
            P("dp"),
            P("dp"),
            P("dp", None),
            P("dp"),
            P("dp", None),
            P("dp"),
            P("dp"),
            P("dp"),
        ),
        check_vma=False,
    )
```

```python
import jax
import jax.numpy as jnp
from jax import lax
from jax.experimental import pallas as pl
from jax.experimental.pallas import tpu as pltpu
from jax.sharding import PartitionSpec as P

HEAD_DIM = 64
DOCS = 8
MOST = 256
BLOCK = 128
WINDOW = 1 + 2 * MOST // BLOCK
LOWEST = -1e30
ROWS = 256
TILE = 512
SWAP = [(0, 1), (1, 0)]


def dense(left, right):
    return jnp.dot(left, right, preferred_element_type=jnp.float32)


def key_windows(segments):
    length = segments.shape[0]
    blocks = segments.reshape(length // BLOCK, BLOCK)
    first = blocks[:, :1]
    last = jnp.minimum(blocks[:, -1:], DOCS - 2)
    before = jnp.sum((segments[None, :] < first).astype(jnp.int32), axis=1)
    upto = jnp.sum((segments[None, :] <= last).astype(jnp.int32), axis=1)
    low = before // BLOCK
    count = jnp.clip((upto + BLOCK - 1) // BLOCK - low, 0, WINDOW)
    count = jnp.where(first[:, 0] == DOCS - 1, 0, count)
    return jnp.minimum(low, length // BLOCK - count), count


def two_heads(pair):
    lane = lax.broadcasted_iota(jnp.int32, pair.shape, 1)
    zero = jnp.zeros_like(pair)
    return jnp.concatenate(
        [jnp.where(lane < HEAD_DIM, pair, zero), jnp.where(lane < HEAD_DIM, zero, pair)], axis=0
    )


def outer_dot(left, right):
    return lax.dot_general(
        left, right, (((1,), (1,)), ((), ())), preferred_element_type=jnp.float32
    )


def own_heads(both):
    return jnp.concatenate([both[:HEAD_DIM, :BLOCK], both[HEAD_DIM:, BLOCK:]], axis=0)


def pair_lanes(pair):
    return slice(pair * BLOCK, pair * BLOCK + BLOCK)


def forward_kernel(
    low_ref, count_ref, seg_row, seg_col, q_ref, k_ref, v_ref, ctx_ref, log_ref, turned
):
    at = pl.program_id(0)
    pairs = q_ref.shape[1] // BLOCK

    @pl.when(at == 0)
    def _():
        turned[...] = v_ref[...].T

    start = pl.multiple_of(low_ref[at] * BLOCK, BLOCK)
    row = seg_row[0]
    valid = row != DOCS - 1
    row = jnp.where(valid, row, -1)

    def work(count):
        window = pl.ds(start, count * BLOCK)
        allowed = seg_col[window, :] == row
        all_scores = []
        for pair in range(pairs):
            lanes = pair_lanes(pair)
            query = two_heads(q_ref[:, lanes] * jnp.bfloat16(0.125))
            all_scores.append(outer_dot(k_ref[window, lanes], query))
        logs = []
        for pair in range(pairs):
            lanes = pair_lanes(pair)
            weights = []
            inverse = []
            for head in range(2):
                own = jnp.where(allowed, all_scores[pair][:, pair_lanes(head)], LOWEST)
                top = jnp.max(own, axis=0, keepdims=True)
                exps = jnp.exp(own - top)
                total = jnp.sum(exps, axis=0, keepdims=True)
                weights.append(exps.astype(jnp.bfloat16))
                inverse.append(jnp.where(valid, 1.0 / total, 0.0))
                logs.append(jnp.where(valid, top + jnp.log(total), -LOWEST))
            both = dense(turned[lanes, window], jnp.concatenate(weights, axis=1))
            both = both * jnp.concatenate(inverse, axis=1)
            ctx_ref[:, lanes] = own_heads(both).T.astype(jnp.bfloat16)
        spare = log_ref.shape[0] - 2 * pairs
        if spare:
            logs.append(jnp.zeros((spare, BLOCK), jnp.float32))
        log_ref[...] = jnp.concatenate(logs, axis=0)

    @pl.when(count_ref[at] == 0)
    def _():
        ctx_ref[...] = jnp.zeros_like(ctx_ref)
        log_ref[...] = jnp.full_like(log_ref, -LOWEST)

    for count in range(1, WINDOW + 1):

        @pl.when(count_ref[at] == count)
        def _():
            work(count)


def backward_kernel(
    low_ref,
    count_ref,
    seg_row,
    seg_col,
    q_ref,
    k_ref,
    v_ref,
    g_ref,
    log_ref,
    dq_ref,
    dk_ref,
    dv_ref,
    sum_ref,
    turned,
    dk_sum,
    dv_sum,
):
    at = pl.program_id(0)
    pairs = q_ref.shape[1] // BLOCK

    @pl.when(at == 0)
    def _():
        turned[...] = k_ref[...].T
        dk_sum[...] = jnp.zeros_like(dk_sum)
        dv_sum[...] = jnp.zeros_like(dv_sum)
        sum_ref[...] = jnp.zeros_like(sum_ref)

    start = pl.multiple_of(low_ref[at] * BLOCK, BLOCK)
    row = seg_row[0]
    row = jnp.where(row != DOCS - 1, row, -1)

    def work(count):
        window = pl.ds(start, count * BLOCK)
        allowed = seg_col[window, :] == row

        def products(pair):
            lanes = pair_lanes(pair)
            query = two_heads(q_ref[:, lanes] * jnp.bfloat16(0.125))
            grad = two_heads(g_ref[:, lanes])
            scores = outer_dot(k_ref[window, lanes], query)
            return query, grad, scores, outer_dot(v_ref[window, lanes], grad)

        def softmax(pair, query, grad, scores, grad_probs):
            probs_low = []
            grad_scores = []
            for head in range(2):
                cols = pair_lanes(head)
                log = log_ref[2 * pair + head : 2 * pair + head + 1, :]
                probs = jnp.exp(jnp.where(allowed, scores[:, cols], LOWEST) - log)
                own = grad_probs[:, cols]
                inner = jnp.sum(probs * own, axis=0, keepdims=True)
                probs_low.append(probs.astype(jnp.bfloat16))
                grad_scores.append((probs * (own - inner)).astype(jnp.bfloat16))
            joined = [jnp.concatenate(p, axis=1) for p in (probs_low, grad_scores)]
            return query, grad, *joined

        def results(pair, query, grad, probs_low, grad_scores):
            lanes = pair_lanes(pair)
            dv_sum[window, lanes] += dense(probs_low, grad)
            dk_sum[window, lanes] += dense(grad_scores, query)
            both = dense(turned[lanes, window], grad_scores)
            query_grad = (own_heads(both).T * 0.125).astype(jnp.bfloat16)
            dq_ref[:, lanes] = query_grad
            sum_ref[0:1, lanes] += column_sum(query_grad)

        ahead = products(0)
        behind = None
        for pair in range(pairs):
            now = ahead
            if pair + 1 < pairs:
                ahead = products(pair + 1)
            done = softmax(pair, *now)
            if pair > 0:
                results(pair - 1, *behind)
            behind = done
        results(pairs - 1, *behind)

    @pl.when(count_ref[at] == 0)
    def _():
        dq_ref[...] = jnp.zeros_like(dq_ref)

    for count in range(1, WINDOW + 1):

        @pl.when(count_ref[at] == count)
        def _():
            work(count)

    @pl.when(at == pl.num_programs(0) - 1)
    def _():
        dk_ref[...] = dk_sum[...].astype(jnp.bfloat16)
        value_grad = dv_sum[...].astype(jnp.bfloat16)
        dv_ref[...] = value_grad
        sum_ref[1:2, :] = column_sum(value_grad)


def attention_call(kernel, name, arrays, outputs, scratch, shape, flops, vmem):
    length, width = shape
    log_rows = width // HEAD_DIM + -(width // HEAD_DIM) % 8
    kinds = {
        "row": (pl.BlockSpec((1, 1, BLOCK), lambda i, *_: (i, 0, 0)), None),
        "col": (pl.BlockSpec((length, BLOCK), lambda i, *_: (0, 0)), None),
        "block": (
            pl.BlockSpec((BLOCK, width), lambda i, *_: (i, 0)),
            jax.ShapeDtypeStruct((length, width), jnp.bfloat16),
        ),
        "whole": (
            pl.BlockSpec((length, width), lambda i, *_: (0, 0)),
            jax.ShapeDtypeStruct((length, width), jnp.bfloat16),
        ),
        "sums": (
            pl.BlockSpec((8, width), lambda i, *_: (0, 0)),
            jax.ShapeDtypeStruct((8, width), jnp.float32),
        ),
        "logs": (
            pl.BlockSpec((log_rows, BLOCK), lambda i, *_: (0, i)),
            jax.ShapeDtypeStruct((log_rows, length), jnp.float32),
        ),
    }
    return pl.pallas_call(
        kernel,
        grid_spec=pltpu.PrefetchScalarGridSpec(
            num_scalar_prefetch=2,
            grid=(length // BLOCK,),
            in_specs=[kinds[k][0] for k in arrays],
            out_specs=[kinds[k][0] for k in outputs],
            scratch_shapes=scratch,
        ),
        out_shape=[kinds[k][1] for k in outputs],
        compiler_params=pltpu.CompilerParams(vmem_limit_bytes=vmem),
        cost_estimate=pl.CostEstimate(
            flops=flops, bytes_accessed=2 * length * width * len(arrays), transcendentals=0
        ),
        name=name,
    )


def attend_forward(query, key, value, segments):
    length, width = query.shape
    call = attention_call(
        forward_kernel,
        "attend_forward",
        ["row", "col", "block", "whole", "whole"],
        ["block", "logs"],
        [pltpu.VMEM((width, length), jnp.bfloat16)],
        (length, width),
        16 * length * width * BLOCK * WINDOW,
        18 << 20,
    )
    return call(*segments, query, key, value)


def attend_backward(query, key, value, segments, grad_context, logs):
    length, width = query.shape
    call = attention_call(
        backward_kernel,
        "attend_backward",
        ["row", "col", "block", "whole", "whole", "block", "logs"],
        ["block", "whole", "whole", "sums"],
        [pltpu.VMEM((width, length), jnp.bfloat16)] + [pltpu.VMEM((length, width), jnp.float32)] * 2,
        (length, width),
        32 * length * width * BLOCK * WINDOW,
        26 << 20,
    )
    return call(*segments, query, key, value, grad_context, logs)


def normalize(summed):
    centre = summed - jnp.mean(summed, axis=-1, keepdims=True)
    scale = lax.rsqrt(jnp.mean(centre * centre, axis=-1, keepdims=True) + 1e-12)
    return centre * scale, scale


def norm_grad(grad, normal, scale):
    mean = jnp.mean(grad, axis=-1, keepdims=True)
    along = jnp.mean(grad * normal, axis=-1, keepdims=True)
    return scale * (grad - mean - normal * along)


def column_sum(array):
    return jnp.sum(array.astype(jnp.float32), axis=0, keepdims=True)


def middle_kernel(core_ref, x_ref, ctx_ref, dy_ref, vec_ref, bias_ref, wo_ref, w1_ref, w2_ref,
                  out_ref, act_ref, low_ref, gom_ref, goo_ref, gim_ref, gio_ref, ga_ref, gc_ref,
                  sum_ref, hid_ref, slope):
    at = pl.program_id(0)
    core = core_ref[0]
    width = x_ref.shape[1]
    hidden = w1_ref.shape[1]
    tiles = [slice(i, i + TILE) for i in range(0, hidden, TILE)]
    out_bias, gain1, shift1, outer_bias, gain2, shift2 = [
        vec_ref[i : i + 1, :].astype(jnp.float32) for i in range(6)
    ]

    @pl.when(at == 0)
    def _():
        sum_ref[...] = jnp.zeros_like(sum_ref)
        hid_ref[...] = jnp.zeros_like(hid_ref)

    first_sum = x_ref[...].astype(jnp.float32) + (dense(ctx_ref[...], wo_ref[...]) + out_bias)
    normal1, scale1 = normalize(first_sum)
    first_norm = normal1 * gain1 + shift1
    low = first_norm.astype(jnp.bfloat16)
    low_ref[...] = low

    def inner_of(tile):
        return dense(low, w1_ref[:, tile]) + bias_ref[:, tile].astype(jnp.float32)

    def gelu(tile, inner):
        below = 0.5 + 0.5 * lax.erf(inner * 0.5**0.5)
        density = jnp.exp(-0.5 * inner * inner) * 0.3989422804014327
        slope[:, tile] = (below + inner * density).astype(jnp.bfloat16)
        act = (inner * below).astype(jnp.bfloat16)
        act_ref[:, tile] = act
        return act

    outer = outer_bias
    ahead = inner_of(tiles[0])
    for i, tile in enumerate(tiles):
        now = ahead
        if i + 1 < len(tiles):
            ahead = inner_of(tiles[i + 1])
        outer = outer + dense(gelu(tile, now), w2_ref[tile, :])
    normal2, scale2 = normalize(first_norm + outer)
    out_ref[...] = (normal2 * gain2 + shift2).astype(jnp.bfloat16)
    dy = dy_ref[...].astype(jnp.float32)
    sum_ref[0:1, :] += column_sum(dy * normal2)
    sum_ref[1:2, :] += column_sum(dy)
    grad_second = norm_grad(dy * gain2, normal2, scale2)
    grad_outer = grad_second.astype(jnp.bfloat16)
    sum_ref[2:3, :] += column_sum(grad_outer)
    left, right = grad_outer[:, : width // 2], grad_outer[:, width // 2 :]
    gom_ref[...] = jnp.where(core == 0, left, right)
    goo_ref[...] = jnp.where(core == 0, right, left)

    grad_norm = grad_second
    ahead = outer_dot(grad_outer, w2_ref[tiles[0], :])
    for i, tile in enumerate(tiles):
        now = ahead
        if i + 1 < len(tiles):
            ahead = outer_dot(grad_outer, w2_ref[tiles[i + 1], :])
        grad = (now * slope[:, tile].astype(jnp.float32)).astype(jnp.bfloat16)
        hid_ref[:, tile] += column_sum(grad)
        slope[:, tile] = grad
        grad_norm = grad_norm + outer_dot(grad, w1_ref[:, tile])
    for index, mine, other in ((0, gim_ref, gio_ref), (1, gio_ref, gim_ref)):

        @pl.when(core == index)
        def _():
            mine[...] = slope[:, : hidden // 2]
            other[...] = slope[:, hidden // 2 :]

    sum_ref[3:4, :] += column_sum(grad_norm * normal1)
    sum_ref[4:5, :] += column_sum(grad_norm)
    grad_attn = norm_grad(grad_norm * gain1, normal1, scale1).astype(jnp.bfloat16)
    sum_ref[5:6, :] += column_sum(grad_attn)
    ga_ref[...] = grad_attn
    gc_ref[...] = outer_dot(grad_attn, wo_ref[...]).astype(jnp.bfloat16)


def middle(core, x, ctx, dy, vec, bias, wo, w1, w2):
    length, width = x.shape
    hidden = w1.shape[1]

    def rows(columns):
        return pl.BlockSpec((ROWS, columns), lambda i, *_: (i, 0))

    def whole(array):
        return pl.BlockSpec(array.shape, lambda i, *_: (0, 0), pipeline_mode=pl.Buffered(1))

    def out(columns):
        return jax.ShapeDtypeStruct((length, columns), jnp.bfloat16)

    outs = [width, hidden, width, width // 2, width // 2, hidden // 2, hidden // 2, width, width]
    return pl.pallas_call(
        middle_kernel,
        grid_spec=pltpu.PrefetchScalarGridSpec(
            num_scalar_prefetch=1,
            grid=(length // ROWS,),
            in_specs=[rows(width)] * 3 + [whole(a) for a in (vec, bias, wo, w1, w2)],
            out_specs=[rows(c) for c in outs] + [pl.BlockSpec((8, width), lambda i, *_: (0, 0)), pl.BlockSpec((1, hidden), lambda i, *_: (0, 0))],
            scratch_shapes=[pltpu.VMEM((ROWS, hidden), jnp.bfloat16)],
        ),
        out_shape=[out(c) for c in outs] + [jax.ShapeDtypeStruct((8, width), jnp.float32), jax.ShapeDtypeStruct((1, hidden), jnp.float32)],
        compiler_params=pltpu.CompilerParams(vmem_limit_bytes=28 << 20),
        cost_estimate=pl.CostEstimate(
            flops=4 * length * width * (width + 2 * hidden),
            bytes_accessed=2 * length * (8 * width + 3 * hidden),
            transcendentals=0,
        ),
        name="middle",
    )(core, x, ctx, dy, vec, bias, wo, w1, w2)


def pick(array, index, axis):
    return lax.dynamic_index_in_dim(array, index, axis, keepdims=False)


def total_of(parts):
    result = parts[0].astype(jnp.float32)
    for part in parts[1:]:
        result = result + part.astype(jnp.float32)
    return result


def tie(*arrays):
    return lax.optimization_barrier(arrays)


def swap(array):
    return lax.ppermute(array, "seq", SWAP)


class Halving:
    def __init__(self, parts, order):
        self.size = lax.axis_size("dp")
        self.me = lax.axis_index("dp")
        bits = self.size.bit_length() - 1
        self.left = list(range(bits - 1, -1, -1))
        self.order = [b for b in order if b < bits] + [b for b in range(bits) if b not in order]
        self.parts = [p.reshape((2,) * bits + p.shape[1:]) for p in parts]
        self.got = None

    def send(self):
        if not self.order:
            return
        bit = self.order.pop(0)
        axis = self.left.index(bit)
        mine = (self.me >> bit) & 1
        sent = total_of([pick(part, 1 - mine, axis) for part in self.parts]).astype(jnp.bfloat16)
        pairs = [(i, i ^ (1 << bit)) for i in range(self.size)]
        self.got = lax.ppermute(sent, "dp", pairs)
        self.parts = [pick(part, mine, axis) for part in self.parts]
        self.left.remove(bit)

    def take(self):
        if self.got is not None:
            self.parts = self.parts + [self.got]
            self.got = None

    def finish(self):
        self.take()
        while self.order:
            self.send()
            self.take()
        return total_of(self.parts)


class Doubling:
    def __init__(self, array):
        self.size = lax.axis_size("dp")
        self.order = list(range(self.size.bit_length() - 1))
        self.total = array
        self.got = None

    def send(self):
        if not self.order:
            return
        bit = self.order.pop(0)
        pairs = [(i, i ^ (1 << bit)) for i in range(self.size)]
        self.sent = self.total.astype(jnp.bfloat16)
        self.got = lax.ppermute(self.sent, "dp", pairs)

    def take(self):
        if self.got is not None:
            self.total = total_of([self.sent, self.got])
            self.got = None

    def finish(self):
        self.take()
        while self.order:
            self.send()
            self.take()
        return self.total


def advance(works, *arrays):
    waiting = [w for w in works if w.got is not None]
    if not waiting and not arrays:
        return []
    out = tie(*[w.got for w in waiting], *arrays)
    for work, got in zip(waiting, out):
        work.got = got
        work.take()
    for work in works:
        work.send()
    return out[len(waiting) :]


def shards(
    tokens,
    segments,
    query_weight,
    query_bias,
    key_weight,
    value_weight,
    value_bias,
    output_weight,
    output_bias,
    first_gain,
    first_shift,
    inner_weight,
    inner_bias,
    outer_weight,
    outer_bias,
    second_gain,
    second_shift,
    cotangent,
):
    rows, half, width = tokens.shape
    core = lax.axis_index("seq")
    size = lax.axis_size("dp")

    def whole_row(array):
        mine = pick(array, core, 0)
        other = lax.ppermute(pick(array, 1 - core, 0), "seq", SWAP)
        first = jnp.where(core == 0, mine, other)
        second = jnp.where(core == 0, other, mine)
        return jnp.concatenate([first, second], axis=0)

    def own_halves(array):
        array = array.reshape(2, half, width)
        mine = pick(array, core, 0)
        other = lax.ppermute(pick(array, 1 - core, 0), "seq", SWAP)
        first = jnp.where(core == 0, mine, other)
        second = jnp.where(core == 0, other, mine)
        return jnp.stack([first, second], axis=0)

    flattened = whole_row(tokens)
    grad_result = whole_row(cotangent)
    segment_row = pick(segments, core, 0)
    query = (dense(flattened, query_weight) + query_bias.astype(jnp.float32)).astype(jnp.bfloat16)
    key = dense(flattened, key_weight).astype(jnp.bfloat16)
    value = (dense(flattened, value_weight) + value_bias.astype(jnp.float32)).astype(jnp.bfloat16)
    length = 2 * half
    place = (
        *key_windows(segment_row),
        segment_row.reshape(length // BLOCK, 1, BLOCK),
        jnp.broadcast_to(segment_row[:, None], (length, BLOCK)),
    )
    context_rows, logsum = attend_forward(query, key, value, place)
    scales = jnp.stack(
        [output_bias, first_gain, first_shift, outer_bias, second_gain, second_shift]
    )
    (
        result,
        act_low,
        norm_low,
        outer_mine,
        outer_other,
        inner_mine,
        inner_other,
        grad_attn,
        grad_context,
        middle_sums,
        inner_bias_term,
    ) = middle(
        core.astype(jnp.int32).reshape(1),
        flattened,
        context_rows,
        grad_result,
        scales,
        inner_bias.reshape(1, -1),
        output_weight,
        inner_weight,
        outer_weight,
    )

    def part_of(array, index):
        columns = array.shape[1] // 2
        return lax.dynamic_slice_in_dim(array, index * columns, columns, axis=1)

    def send_part(left, right):
        return dense(left.T, right).astype(jnp.bfloat16)

    outer_sent, outer_mine, inner_other = tie(
        send_part(act_low, outer_other), outer_mine, inner_other
    )
    outer_got = swap(outer_sent)
    inner_sent, outer_mine = tie(send_part(norm_low, inner_other), outer_mine)
    inner_got = swap(inner_sent)
    outer_kept = dense(act_low.T, outer_mine)
    output_sent = send_part(context_rows, part_of(grad_attn, 1 - core))
    outer_got, outer_kept, output_sent, inner_mine = tie(
        outer_got, outer_kept, output_sent, inner_mine
    )
    output_got = swap(output_sent)
    own = width // size
    quarter = width // 2

    first_work = Halving(
        [p.reshape(size, 4 * own, -1)[:, : 3 * own] for p in (outer_kept, outer_got)], (0, 1, 2, 3)
    )
    first_work.send()
    inner_kept = dense(norm_low.T, inner_mine)
    output_kept = dense(context_rows.T, part_of(grad_attn, core))
    inner_got, inner_kept, output_got, output_kept, grad_context = tie(
        inner_got, inner_kept, output_got, output_kept, grad_context
    )
    second_work = Halving(
        [p.reshape(size, own, -1)[:, :, : 3 * quarter] for p in (inner_kept, inner_got)],
        (2, 0, 1, 3),
    )
    second_work.send()
    third_work = Halving(
        [
            jnp.concatenate(
                [
                    outer.reshape(size, 4 * own, -1)[:, 3 * own :],
                    inner.reshape(size, own, -1)[:, :, 3 * quarter :],
                    output.reshape(size, own, -1),
                ],
                axis=1,
            )
            for outer, inner, output in (
                (outer_kept.astype(jnp.bfloat16), inner_kept.astype(jnp.bfloat16), output_kept.astype(jnp.bfloat16)),
                (outer_got, inner_got, output_got),
            )
        ],
        (1, 2, 0, 3),
    )
    third_work.send()
    early = [first_work, second_work, third_work]
    grad_query, grad_key, grad_value, attention_sums = attend_backward(
        query, key, value, place, grad_context, logsum
    )
    three = (grad_query, grad_key, grad_value)
    others = [send_part(flattened, part_of(g, 1 - core)) for g in three]
    small = jnp.concatenate(
        [attention_sums[:2], middle_sums[:6], inner_bias_term.reshape(-1, width)], axis=0
    )
    small = jnp.pad(small, ((0, -small.shape[0] % 16), (0, 0)))
    small_low = small.astype(jnp.bfloat16)
    layer_out = own_halves(result)
    out = advance(early, *others, small_low, layer_out, *three)
    others_got = [swap(o) for o in others]
    small_low, layer_out, three = out[3], out[4], out[5:]
    small_other = swap(small_low)
    kept = [dense(flattened.T, part_of(g, core)) for g in three]
    out = tie(*others_got, small_other, *kept, *three)
    others_got, small_other, kept, three = out[:3], out[3], out[4:7], out[7:]
    small_work = Doubling(total_of([small_low, small_other]))
    late = []
    for mine, got, order in zip(kept, others_got, [(0, 1, 2, 3), (1, 2, 0, 3), (2, 0, 1, 3)]):
        work = Halving([p.reshape(size, own, -1) for p in (mine, got)], order)
        work.send()
        late.append(work)
    small_work.send()
    tokens_grad = grad_attn.astype(jnp.float32)
    for grad, weight in zip(three, (query_weight, key_weight, value_weight)):
        tokens_grad = tokens_grad + dense(grad, weight.T)
    works = early + late + [small_work]
    (tokens_grad,) = advance(works, tokens_grad.astype(jnp.bfloat16))
    tokens_grad = own_halves(tokens_grad)

    def both_halves(half):
        other = swap(half)
        first = jnp.where(core == 0, half, other)
        second = jnp.where(core == 0, other, half)
        return jnp.concatenate([first, second], axis=1)

    (tokens_grad,) = advance(works, tokens_grad)
    while any(work.order for work in early):
        advance(works)
    advance([work for work in early if work.got is not None])
    first_sum, second_sum, third_sum = [work.finish() for work in early]
    outer_weight_grad = both_halves(jnp.concatenate([first_sum, third_sum[:own]], axis=0))
    inner_weight_grad = both_halves(
        jnp.concatenate([second_sum, third_sum[own : 2 * own]], axis=1)
    )
    output_weight_grad = both_halves(third_sum[2 * own :])
    outer_weight_grad, inner_weight_grad, output_weight_grad = advance(
        late + [small_work], outer_weight_grad, inner_weight_grad, output_weight_grad
    )
    while any(work.order for work in late + [small_work]):
        advance(late + [small_work])
    advance([work for work in late + [small_work] if work.got is not None])
    query_weight_grad, key_weight_grad, value_weight_grad = [
        both_halves(work.finish()) for work in late
    ]
    sums = small_work.finish()
    me = lax.axis_index("dp")
    own_sums = lax.dynamic_slice_in_dim(sums, me * own, own, axis=1)
    (
        query_bias_grad,
        value_bias_grad,
        second_gain_grad,
        second_shift_grad,
        outer_bias_grad,
        first_gain_grad,
        first_shift_grad,
        output_bias_grad,
    ) = [own_sums[i] for i in range(8)]
    wide = inner_bias.shape[0] // size
    per_row = width // wide
    inner_bias_grad = lax.dynamic_slice(
        sums, (8 + me // per_row, me % per_row * wide), (1, wide)
    ).reshape(-1)
    return (
        layer_out,
        tokens_grad,
        query_weight_grad,
        query_bias_grad,
        key_weight_grad,
        value_weight_grad,
        value_bias_grad,
        output_weight_grad,
        output_bias_grad,
        first_gain_grad,
        first_shift_grad,
        inner_weight_grad,
        inner_bias_grad,
        outer_weight_grad,
        outer_bias_grad,
        second_gain_grad,
        second_shift_grad,
    )


def solution(mesh):
    split = P("dp", "seq", None)
    return jax.shard_map(
        shards,
        mesh=mesh,
        in_specs=(split, P("dp", None)) + (P(),) * 15 + (split,),
        out_specs=(
            split,
            split,
            P("dp", None),
            P("dp"),
            P("dp", None),
            P("dp", None),
            P("dp"),
            P("dp", None),
            P("dp"),
            P("dp"),
            P("dp"),
            P("dp", None),
            P("dp"),
            P("dp", None),
            P("dp"),
            P("dp"),
            P("dp"),
        ),
        check_vma=False,
    )
```

```python
import jax
import jax.numpy as jnp
from jax import lax
from jax.experimental import pallas as pl
from jax.experimental.pallas import tpu as pltpu
from jax.sharding import PartitionSpec as P

HEAD_DIM = 64
DOCS = 8
MOST = 256
BLOCK = 128
WINDOW = 1 + 2 * MOST // BLOCK
LOWEST = -1e30
ROWS = 256
TILE = 512
SWAP = [(0, 1), (1, 0)]


def dense(left, right):
    return jnp.dot(left, right, preferred_element_type=jnp.float32)


def key_windows(segments):
    length = segments.shape[0]
    blocks = segments.reshape(length // BLOCK, BLOCK)
    first = blocks[:, :1]
    last = jnp.minimum(blocks[:, -1:], DOCS - 2)
    before = jnp.sum((segments[None, :] < first).astype(jnp.int32), axis=1)
    upto = jnp.sum((segments[None, :] <= last).astype(jnp.int32), axis=1)
    low = before // BLOCK
    count = jnp.clip((upto + BLOCK - 1) // BLOCK - low, 0, WINDOW)
    count = jnp.where(first[:, 0] == DOCS - 1, 0, count)
    return jnp.minimum(low, length // BLOCK - count), count


def two_heads(pair):
    lane = lax.broadcasted_iota(jnp.int32, pair.shape, 1)
    zero = jnp.zeros_like(pair)
    return jnp.concatenate(
        [jnp.where(lane < HEAD_DIM, pair, zero), jnp.where(lane < HEAD_DIM, zero, pair)], axis=0
    )


def outer_dot(left, right):
    return lax.dot_general(
        left, right, (((1,), (1,)), ((), ())), preferred_element_type=jnp.float32
    )


def own_heads(both):
    return jnp.concatenate([both[:HEAD_DIM, :BLOCK], both[HEAD_DIM:, BLOCK:]], axis=0)


def pair_lanes(pair):
    return slice(pair * BLOCK, pair * BLOCK + BLOCK)


def forward_kernel(
    low_ref, count_ref, seg_row, seg_col, q_ref, k_ref, v_ref, ctx_ref, log_ref, turned
):
    at = pl.program_id(0)
    pairs = q_ref.shape[1] // BLOCK

    @pl.when(at == 0)
    def _():
        turned[...] = v_ref[...].T

    start = pl.multiple_of(low_ref[at] * BLOCK, BLOCK)
    row = seg_row[0]
    valid = row != DOCS - 1
    row = jnp.where(valid, row, -1)

    def work(count):
        window = pl.ds(start, count * BLOCK)
        allowed = seg_col[window, :] == row
        all_scores = []
        for pair in range(pairs):
            lanes = pair_lanes(pair)
            query = two_heads(q_ref[:, lanes] * jnp.bfloat16(0.125))
            all_scores.append(outer_dot(k_ref[window, lanes], query))
        logs = []
        for pair in range(pairs):
            lanes = pair_lanes(pair)
            weights = []
            inverse = []
            for head in range(2):
                own = jnp.where(allowed, all_scores[pair][:, pair_lanes(head)], LOWEST)
                top = jnp.max(own, axis=0, keepdims=True)
                exps = jnp.exp(own - top)
                total = jnp.sum(exps, axis=0, keepdims=True)
                weights.append(exps.astype(jnp.bfloat16))
                inverse.append(jnp.where(valid, 1.0 / total, 0.0))
                logs.append(jnp.where(valid, top + jnp.log(total), -LOWEST))
            both = dense(turned[lanes, window], jnp.concatenate(weights, axis=1))
            both = both * jnp.concatenate(inverse, axis=1)
            ctx_ref[:, lanes] = own_heads(both).T.astype(jnp.bfloat16)
        spare = log_ref.shape[0] - 2 * pairs
        if spare:
            logs.append(jnp.zeros((spare, BLOCK), jnp.float32))
        log_ref[...] = jnp.concatenate(logs, axis=0)

    @pl.when(count_ref[at] == 0)
    def _():
        ctx_ref[...] = jnp.zeros_like(ctx_ref)
        log_ref[...] = jnp.full_like(log_ref, -LOWEST)

    for count in range(1, WINDOW + 1):

        @pl.when(count_ref[at] == count)
        def _():
            work(count)


def backward_kernel(
    low_ref,
    count_ref,
    seg_row,
    seg_col,
    q_ref,
    k_ref,
    v_ref,
    g_ref,
    log_ref,
    dq_ref,
    dk_ref,
    dv_ref,
    sum_ref,
    turned,
    dk_sum,
    dv_sum,
):
    at = pl.program_id(0)
    pairs = q_ref.shape[1] // BLOCK

    @pl.when(at == 0)
    def _():
        turned[...] = k_ref[...].T
        dk_sum[...] = jnp.zeros_like(dk_sum)
        dv_sum[...] = jnp.zeros_like(dv_sum)
        sum_ref[...] = jnp.zeros_like(sum_ref)

    start = pl.multiple_of(low_ref[at] * BLOCK, BLOCK)
    row = seg_row[0]
    row = jnp.where(row != DOCS - 1, row, -1)

    def work(count):
        window = pl.ds(start, count * BLOCK)
        allowed = seg_col[window, :] == row

        def products(pair):
            lanes = pair_lanes(pair)
            query = two_heads(q_ref[:, lanes] * jnp.bfloat16(0.125))
            grad = two_heads(g_ref[:, lanes])
            scores = outer_dot(k_ref[window, lanes], query)
            return query, grad, scores, outer_dot(v_ref[window, lanes], grad)

        def softmax(pair, query, grad, scores, grad_probs):
            probs_low = []
            grad_scores = []
            for head in range(2):
                cols = pair_lanes(head)
                log = log_ref[2 * pair + head : 2 * pair + head + 1, :]
                probs = jnp.exp(jnp.where(allowed, scores[:, cols], LOWEST) - log)
                own = grad_probs[:, cols]
                inner = jnp.sum(probs * own, axis=0, keepdims=True)
                probs_low.append(probs.astype(jnp.bfloat16))
                grad_scores.append((probs * (own - inner)).astype(jnp.bfloat16))
            joined = [jnp.concatenate(p, axis=1) for p in (probs_low, grad_scores)]
            return query, grad, *joined

        def results(pair, query, grad, probs_low, grad_scores):
            lanes = pair_lanes(pair)
            dv_sum[window, lanes] += dense(probs_low, grad)
            dk_sum[window, lanes] += dense(grad_scores, query)
            both = dense(turned[lanes, window], grad_scores)
            query_grad = (own_heads(both).T * 0.125).astype(jnp.bfloat16)
            dq_ref[:, lanes] = query_grad
            sum_ref[0:1, lanes] += column_sum(query_grad)

        ahead = products(0)
        behind = None
        for pair in range(pairs):
            now = ahead
            if pair + 1 < pairs:
                ahead = products(pair + 1)
            done = softmax(pair, *now)
            if pair > 0:
                results(pair - 1, *behind)
            behind = done
        results(pairs - 1, *behind)

    @pl.when(count_ref[at] == 0)
    def _():
        dq_ref[...] = jnp.zeros_like(dq_ref)

    for count in range(1, WINDOW + 1):

        @pl.when(count_ref[at] == count)
        def _():
            work(count)

    @pl.when(at == pl.num_programs(0) - 1)
    def _():
        dk_ref[...] = dk_sum[...].astype(jnp.bfloat16)
        value_grad = dv_sum[...].astype(jnp.bfloat16)
        dv_ref[...] = value_grad
        sum_ref[1:2, :] = column_sum(value_grad)


def attention_call(kernel, name, arrays, outputs, scratch, shape, flops, vmem):
    length, width = shape
    log_rows = width // HEAD_DIM + -(width // HEAD_DIM) % 8
    kinds = {
        "row": (pl.BlockSpec((1, 1, BLOCK), lambda i, *_: (i, 0, 0)), None),
        "col": (pl.BlockSpec((length, BLOCK), lambda i, *_: (0, 0)), None),
        "block": (
            pl.BlockSpec((BLOCK, width), lambda i, *_: (i, 0)),
            jax.ShapeDtypeStruct((length, width), jnp.bfloat16),
        ),
        "whole": (
            pl.BlockSpec((length, width), lambda i, *_: (0, 0)),
            jax.ShapeDtypeStruct((length, width), jnp.bfloat16),
        ),
        "sums": (
            pl.BlockSpec((8, width), lambda i, *_: (0, 0)),
            jax.ShapeDtypeStruct((8, width), jnp.float32),
        ),
        "logs": (
            pl.BlockSpec((log_rows, BLOCK), lambda i, *_: (0, i)),
            jax.ShapeDtypeStruct((log_rows, length), jnp.float32),
        ),
    }
    return pl.pallas_call(
        kernel,
        grid_spec=pltpu.PrefetchScalarGridSpec(
            num_scalar_prefetch=2,
            grid=(length // BLOCK,),
            in_specs=[kinds[k][0] for k in arrays],
            out_specs=[kinds[k][0] for k in outputs],
            scratch_shapes=scratch,
        ),
        out_shape=[kinds[k][1] for k in outputs],
        compiler_params=pltpu.CompilerParams(vmem_limit_bytes=vmem),
        cost_estimate=pl.CostEstimate(
            flops=flops, bytes_accessed=2 * length * width * len(arrays), transcendentals=0
        ),
        name=name,
    )


def attend_forward(query, key, value, segments):
    length, width = query.shape
    call = attention_call(
        forward_kernel,
        "attend_forward",
        ["row", "col", "block", "whole", "whole"],
        ["block", "logs"],
        [pltpu.VMEM((width, length), jnp.bfloat16)],
        (length, width),
        16 * length * width * BLOCK * WINDOW,
        18 << 20,
    )
    return call(*segments, query, key, value)


def attend_backward(query, key, value, segments, grad_context, logs):
    length, width = query.shape
    call = attention_call(
        backward_kernel,
        "attend_backward",
        ["row", "col", "block", "whole", "whole", "block", "logs"],
        ["block", "whole", "whole", "sums"],
        [pltpu.VMEM((width, length), jnp.bfloat16)] + [pltpu.VMEM((length, width), jnp.float32)] * 2,
        (length, width),
        32 * length * width * BLOCK * WINDOW,
        26 << 20,
    )
    return call(*segments, query, key, value, grad_context, logs)


def normalize(summed):
    centre = summed - jnp.mean(summed, axis=-1, keepdims=True)
    scale = lax.rsqrt(jnp.mean(centre * centre, axis=-1, keepdims=True) + 1e-12)
    return centre * scale, scale


def norm_grad(grad, normal, scale):
    mean = jnp.mean(grad, axis=-1, keepdims=True)
    along = jnp.mean(grad * normal, axis=-1, keepdims=True)
    return scale * (grad - mean - normal * along)


def column_sum(array):
    return jnp.sum(array.astype(jnp.float32), axis=0, keepdims=True)


def middle_kernel(core_ref, x_ref, ctx_ref, dy_ref, vec_ref, bias_ref, wo_ref, w1_ref, w2_ref,
                  out_ref, act_ref, low_ref, gom_ref, goo_ref, gim_ref, gio_ref, ga_ref, gc_ref,
                  sum_ref, hid_ref, slope):
    at = pl.program_id(0)
    core = core_ref[0]
    width = x_ref.shape[1]
    hidden = w1_ref.shape[1]
    tiles = [slice(i, i + TILE) for i in range(0, hidden, TILE)]
    out_bias, gain1, shift1, outer_bias, gain2, shift2 = [
        vec_ref[i : i + 1, :].astype(jnp.float32) for i in range(6)
    ]

    @pl.when(at == 0)
    def _():
        sum_ref[...] = jnp.zeros_like(sum_ref)
        hid_ref[...] = jnp.zeros_like(hid_ref)

    first_sum = x_ref[...].astype(jnp.float32) + (dense(ctx_ref[...], wo_ref[...]) + out_bias)
    normal1, scale1 = normalize(first_sum)
    first_norm = normal1 * gain1 + shift1
    low = first_norm.astype(jnp.bfloat16)
    low_ref[...] = low

    def inner_of(tile):
        return dense(low, w1_ref[:, tile]) + bias_ref[:, tile].astype(jnp.float32)

    def gelu(tile, inner):
        below = 0.5 + 0.5 * lax.erf(inner * 0.5**0.5)
        density = jnp.exp(-0.5 * inner * inner) * 0.3989422804014327
        slope[:, tile] = (below + inner * density).astype(jnp.bfloat16)
        act = (inner * below).astype(jnp.bfloat16)
        act_ref[:, tile] = act
        return act

    outer = outer_bias
    ahead = inner_of(tiles[0])
    for i, tile in enumerate(tiles):
        now = ahead
        if i + 1 < len(tiles):
            ahead = inner_of(tiles[i + 1])
        outer = outer + dense(gelu(tile, now), w2_ref[tile, :])
    normal2, scale2 = normalize(first_norm + outer)
    out_ref[...] = (normal2 * gain2 + shift2).astype(jnp.bfloat16)
    dy = dy_ref[...].astype(jnp.float32)
    sum_ref[0:1, :] += column_sum(dy * normal2)
    sum_ref[1:2, :] += column_sum(dy)
    grad_second = norm_grad(dy * gain2, normal2, scale2)
    grad_outer = grad_second.astype(jnp.bfloat16)
    sum_ref[2:3, :] += column_sum(grad_outer)
    left, right = grad_outer[:, : width // 2], grad_outer[:, width // 2 :]
    gom_ref[...] = jnp.where(core == 0, left, right)
    goo_ref[...] = jnp.where(core == 0, right, left)

    grad_norm = grad_second
    ahead = outer_dot(grad_outer, w2_ref[tiles[0], :])
    for i, tile in enumerate(tiles):
        now = ahead
        if i + 1 < len(tiles):
            ahead = outer_dot(grad_outer, w2_ref[tiles[i + 1], :])
        grad = (now * slope[:, tile].astype(jnp.float32)).astype(jnp.bfloat16)
        hid_ref[:, tile] += column_sum(grad)
        slope[:, tile] = grad
        grad_norm = grad_norm + outer_dot(grad, w1_ref[:, tile])
    for index, mine, other in ((0, gim_ref, gio_ref), (1, gio_ref, gim_ref)):

        @pl.when(core == index)
        def _():
            mine[...] = slope[:, : hidden // 2]
            other[...] = slope[:, hidden // 2 :]

    sum_ref[3:4, :] += column_sum(grad_norm * normal1)
    sum_ref[4:5, :] += column_sum(grad_norm)
    grad_attn = norm_grad(grad_norm * gain1, normal1, scale1).astype(jnp.bfloat16)
    sum_ref[5:6, :] += column_sum(grad_attn)
    ga_ref[...] = grad_attn
    gc_ref[...] = outer_dot(grad_attn, wo_ref[...]).astype(jnp.bfloat16)


def middle(core, x, ctx, dy, vec, bias, wo, w1, w2):
    length, width = x.shape
    hidden = w1.shape[1]

    def rows(columns):
        return pl.BlockSpec((ROWS, columns), lambda i, *_: (i, 0))

    def whole(array):
        return pl.BlockSpec(array.shape, lambda i, *_: (0, 0), pipeline_mode=pl.Buffered(1))

    def out(columns):
        return jax.ShapeDtypeStruct((length, columns), jnp.bfloat16)

    outs = [width, hidden, width, width // 2, width // 2, hidden // 2, hidden // 2, width, width]
    return pl.pallas_call(
        middle_kernel,
        grid_spec=pltpu.PrefetchScalarGridSpec(
            num_scalar_prefetch=1,
            grid=(length // ROWS,),
            in_specs=[rows(width)] * 3 + [whole(a) for a in (vec, bias, wo, w1, w2)],
            out_specs=[rows(c) for c in outs] + [pl.BlockSpec((8, width), lambda i, *_: (0, 0)), pl.BlockSpec((1, hidden), lambda i, *_: (0, 0))],
            scratch_shapes=[pltpu.VMEM((ROWS, hidden), jnp.bfloat16)],
        ),
        out_shape=[out(c) for c in outs] + [jax.ShapeDtypeStruct((8, width), jnp.float32), jax.ShapeDtypeStruct((1, hidden), jnp.float32)],
        compiler_params=pltpu.CompilerParams(vmem_limit_bytes=28 << 20),
        cost_estimate=pl.CostEstimate(
            flops=4 * length * width * (width + 2 * hidden),
            bytes_accessed=2 * length * (8 * width + 3 * hidden),
            transcendentals=0,
        ),
        name="middle",
    )(core, x, ctx, dy, vec, bias, wo, w1, w2)


def pick(array, index, axis):
    return lax.dynamic_index_in_dim(array, index, axis, keepdims=False)


def total_of(parts):
    result = parts[0].astype(jnp.float32)
    for part in parts[1:]:
        result = result + part.astype(jnp.float32)
    return result


def tie(*arrays):
    return lax.optimization_barrier(arrays)


def swap(array):
    return lax.ppermute(array, "seq", SWAP)


class Halving:
    def __init__(self, parts, order):
        self.size = lax.axis_size("dp")
        self.me = lax.axis_index("dp")
        bits = self.size.bit_length() - 1
        self.left = list(range(bits - 1, -1, -1))
        self.order = [b for b in order if b < bits] + [b for b in range(bits) if b not in order]
        self.parts = [p.reshape((2,) * bits + p.shape[1:]) for p in parts]
        self.got = None

    def send(self):
        if not self.order:
            return
        bit = self.order.pop(0)
        axis = self.left.index(bit)
        mine = (self.me >> bit) & 1
        sent = total_of([pick(part, 1 - mine, axis) for part in self.parts]).astype(jnp.bfloat16)
        pairs = [(i, i ^ (1 << bit)) for i in range(self.size)]
        self.got = lax.ppermute(sent, "dp", pairs)
        self.parts = [pick(part, mine, axis) for part in self.parts]
        self.left.remove(bit)

    def take(self):
        if self.got is not None:
            self.parts = self.parts + [self.got]
            self.got = None

    def finish(self):
        self.take()
        while self.order:
            self.send()
            self.take()
        return total_of(self.parts)


class Doubling:
    def __init__(self, array):
        self.size = lax.axis_size("dp")
        self.order = list(range(self.size.bit_length() - 1))
        self.total = array
        self.got = None

    def send(self):
        if not self.order:
            return
        bit = self.order.pop(0)
        pairs = [(i, i ^ (1 << bit)) for i in range(self.size)]
        self.sent = self.total.astype(jnp.bfloat16)
        self.got = lax.ppermute(self.sent, "dp", pairs)

    def take(self):
        if self.got is not None:
            self.total = total_of([self.sent, self.got])
            self.got = None

    def finish(self):
        self.take()
        while self.order:
            self.send()
            self.take()
        return self.total


def advance(works, *arrays):
    waiting = [w for w in works if w.got is not None]
    if not waiting and not arrays:
        return []
    out = tie(*[w.got for w in waiting], *arrays)
    for work, got in zip(waiting, out):
        work.got = got
        work.take()
    for work in works:
        work.send()
    return out[len(waiting) :]


def shards(
    tokens,
    segments,
    query_weight,
    query_bias,
    key_weight,
    value_weight,
    value_bias,
    output_weight,
    output_bias,
    first_gain,
    first_shift,
    inner_weight,
    inner_bias,
    outer_weight,
    outer_bias,
    second_gain,
    second_shift,
    cotangent,
):
    rows, half, width = tokens.shape
    core = lax.axis_index("seq")
    size = lax.axis_size("dp")

    def whole_row(array):
        mine = pick(array, core, 0)
        other = lax.ppermute(pick(array, 1 - core, 0), "seq", SWAP)
        first = jnp.where(core == 0, mine, other)
        second = jnp.where(core == 0, other, mine)
        return jnp.concatenate([first, second], axis=0)

    def own_halves(array):
        array = array.reshape(2, half, width)
        mine = pick(array, core, 0)
        other = lax.ppermute(pick(array, 1 - core, 0), "seq", SWAP)
        first = jnp.where(core == 0, mine, other)
        second = jnp.where(core == 0, other, mine)
        return jnp.stack([first, second], axis=0)

    flattened = whole_row(tokens)
    grad_result = whole_row(cotangent)
    segment_row = pick(segments, core, 0)
    query = (dense(flattened, query_weight) + query_bias.astype(jnp.float32)).astype(jnp.bfloat16)
    key = dense(flattened, key_weight).astype(jnp.bfloat16)
    value = (dense(flattened, value_weight) + value_bias.astype(jnp.float32)).astype(jnp.bfloat16)
    length = 2 * half
    place = (
        *key_windows(segment_row),
        segment_row.reshape(length // BLOCK, 1, BLOCK),
        jnp.broadcast_to(segment_row[:, None], (length, BLOCK)),
    )
    context_rows, logsum = attend_forward(query, key, value, place)
    scales = jnp.stack(
        [output_bias, first_gain, first_shift, outer_bias, second_gain, second_shift]
    )
    (
        result,
        act_low,
        norm_low,
        outer_mine,
        outer_other,
        inner_mine,
        inner_other,
        grad_attn,
        grad_context,
        middle_sums,
        inner_bias_term,
    ) = middle(
        core.astype(jnp.int32).reshape(1),
        flattened,
        context_rows,
        grad_result,
        scales,
        inner_bias.reshape(1, -1),
        output_weight,
        inner_weight,
        outer_weight,
    )

    def part_of(array, index):
        columns = array.shape[1] // 2
        return lax.dynamic_slice_in_dim(array, index * columns, columns, axis=1)

    def send_part(left, right):
        return dense(left.T, right).astype(jnp.bfloat16)

    outer_sent, outer_mine, inner_other = tie(
        send_part(act_low, outer_other), outer_mine, inner_other
    )
    outer_got = swap(outer_sent)
    inner_sent, outer_mine = tie(send_part(norm_low, inner_other), outer_mine)
    inner_got = swap(inner_sent)
    outer_kept = dense(act_low.T, outer_mine)
    output_sent = send_part(context_rows, part_of(grad_attn, 1 - core))
    outer_got, outer_kept, output_sent, inner_mine = tie(
        outer_got, outer_kept, output_sent, inner_mine
    )
    output_got = swap(output_sent)
    own = width // size
    quarter = width // 2

    first_work = Halving(
        [p.reshape(size, 4 * own, -1)[:, : 3 * own] for p in (outer_kept, outer_got)], (0, 1, 2, 3)
    )
    first_work.send()
    inner_kept = dense(norm_low.T, inner_mine)
    output_kept = dense(context_rows.T, part_of(grad_attn, core))
    inner_got, inner_kept, output_got, output_kept, grad_context = tie(
        inner_got, inner_kept, output_got, output_kept, grad_context
    )
    second_work = Halving(
        [p.reshape(size, own, -1)[:, :, : 3 * quarter] for p in (inner_kept, inner_got)],
        (2, 0, 1, 3),
    )
    second_work.send()
    third_work = Halving(
        [
            jnp.concatenate(
                [
                    outer.reshape(size, 4 * own, -1)[:, 3 * own :],
                    inner.reshape(size, own, -1)[:, :, 3 * quarter :],
                    output.reshape(size, own, -1),
                ],
                axis=1,
            )
            for outer, inner, output in (
                (outer_kept.astype(jnp.bfloat16), inner_kept.astype(jnp.bfloat16), output_kept.astype(jnp.bfloat16)),
                (outer_got, inner_got, output_got),
            )
        ],
        (1, 2, 0, 3),
    )
    third_work.send()
    early = [first_work, second_work, third_work]
    grad_query, grad_key, grad_value, attention_sums = attend_backward(
        query, key, value, place, grad_context, logsum
    )
    three = (grad_query, grad_key, grad_value)
    others = [send_part(flattened, part_of(g, 1 - core)) for g in three]
    small = jnp.concatenate(
        [attention_sums[:2], middle_sums[:6], inner_bias_term.reshape(-1, width)], axis=0
    )
    small = jnp.pad(small, ((0, -small.shape[0] % 16), (0, 0)))
    small_low = small.astype(jnp.bfloat16)
    out = advance(early, *others, small_low, result, *three)
    others_got = [swap(o) for o in others]
    small_low, result, three = out[3], out[4], out[5:]
    small_other = swap(small_low)
    kept = [dense(flattened.T, part_of(g, core)) for g in three]
    out = tie(*others_got, small_other, *kept, *three)
    others_got, small_other, kept, three = out[:3], out[3], out[4:7], out[7:]
    small_work = Doubling(total_of([small_low, small_other]))
    late = []
    for mine, got, order in zip(kept, others_got, [(0, 1, 2, 3), (1, 2, 0, 3), (2, 0, 1, 3)]):
        work = Halving([p.reshape(size, own, -1) for p in (mine, got)], order)
        work.send()
        late.append(work)
    small_work.send()
    tokens_grad = grad_attn.astype(jnp.float32)
    for grad, weight in zip(three, (query_weight, key_weight, value_weight)):
        tokens_grad = tokens_grad + dense(grad, weight.T)
    works = early + late + [small_work]
    tokens_grad, result = advance(works, tokens_grad.astype(jnp.bfloat16), result)
    layer_out = own_halves(result)
    tokens_grad = own_halves(tokens_grad)

    def both_halves(half):
        other = swap(half)
        first = jnp.where(core == 0, half, other)
        second = jnp.where(core == 0, other, half)
        return jnp.concatenate([first, second], axis=1)

    tokens_grad, layer_out = advance(works, tokens_grad, layer_out)
    while any(work.order for work in early):
        advance(works)
    advance([work for work in early if work.got is not None])
    first_sum, second_sum, third_sum = [work.finish() for work in early]
    outer_weight_grad = both_halves(jnp.concatenate([first_sum, third_sum[:own]], axis=0))
    inner_weight_grad = both_halves(
        jnp.concatenate([second_sum, third_sum[own : 2 * own]], axis=1)
    )
    output_weight_grad = both_halves(third_sum[2 * own :])
    outer_weight_grad, inner_weight_grad, output_weight_grad = advance(
        late + [small_work], outer_weight_grad, inner_weight_grad, output_weight_grad
    )
    while any(work.order for work in late + [small_work]):
        advance(late + [small_work])
    advance([work for work in late + [small_work] if work.got is not None])
    query_weight_grad, key_weight_grad, value_weight_grad = [
        both_halves(work.finish()) for work in late
    ]
    sums = small_work.finish()
    me = lax.axis_index("dp")
    own_sums = lax.dynamic_slice_in_dim(sums, me * own, own, axis=1)
    (
        query_bias_grad,
        value_bias_grad,
        second_gain_grad,
        second_shift_grad,
        outer_bias_grad,
        first_gain_grad,
        first_shift_grad,
        output_bias_grad,
    ) = [own_sums[i] for i in range(8)]
    wide = inner_bias.shape[0] // size
    per_row = width // wide
    inner_bias_grad = lax.dynamic_slice(
        sums, (8 + me // per_row, me % per_row * wide), (1, wide)
    ).reshape(-1)
    return (
        layer_out,
        tokens_grad,
        query_weight_grad,
        query_bias_grad,
        key_weight_grad,
        value_weight_grad,
        value_bias_grad,
        output_weight_grad,
        output_bias_grad,
        first_gain_grad,
        first_shift_grad,
        inner_weight_grad,
        inner_bias_grad,
        outer_weight_grad,
        outer_bias_grad,
        second_gain_grad,
        second_shift_grad,
    )


def solution(mesh):
    split = P("dp", "seq", None)
    return jax.shard_map(
        shards,
        mesh=mesh,
        in_specs=(split, P("dp", None)) + (P(),) * 15 + (split,),
        out_specs=(
            split,
            split,
            P("dp", None),
            P("dp"),
            P("dp", None),
            P("dp", None),
            P("dp"),
            P("dp", None),
            P("dp"),
            P("dp"),
            P("dp"),
            P("dp", None),
            P("dp"),
            P("dp", None),
            P("dp"),
            P("dp"),
            P("dp"),
        ),
        check_vma=False,
    )
```
